256 devices in a mesh: seq: 32 (over x, z), tensor: 8 (over y, core).
Axes of the slice: x: 4, y: 4, z: 8, core: 2. Of those that a mesh axis runs over, the one named last changes fastest.
Arguments:
- prefill_x: bfloat16 [8192, 4096], P('seq'), may hold values from -8 to 8
- decode_x: bfloat16 [64, 4096], P('seq'), may hold values from -6 to 6
- ln_gain: float32 [4096], replicated, may hold values from 0.1 to 1.9
- ln_bias: float32 [4096], replicated, may hold values from -1.75 to 1.75
- wqkv: bfloat16 [4096, 16, 3, 128], P(None, 'tensor'), may hold values from -0.09375 to 0.09375
- qkv_bias: float32 [16, 3, 128], P('tensor'), may hold values from -3 to 3
- dense_w: bfloat16 [16, 128, 4096], P('tensor'), may hold values from -0.125 to 0.125
- dense_bias: float32 [4096], P('tensor'), may hold values from -3 to 3
- kv_cache: bfloat16 [2, 25600, 16, 128], P(None, 'seq', 'tensor'), may hold values from -1000 to 1000
- slot_owner: int32 [25600], P('seq'), may hold values from -1 to 74, as said below
- group_of: int32 [64], replicated, may hold values from 0 to 7
- span_lens: int32 [3], replicated, may hold values from 1 to 4096, 8192 in all
Outputs:
- prefill_out: bfloat16 [8192, 4096], P('seq', 'tensor')
- decode_out: bfloat16 [64, 4096], P('seq', 'tensor')
The draws below stay inside these ranges and needn't reach their ends.
Inputs may be any that keep to these rules, and one draw needn't show every extreme that they name: `slot_owner`: the slots of one sequence form one run of whole pages of 16 slots, runs in increasing order of sequence number; empty slots lie only at the end of a run's last page. Sequences 0 .. 2 are the spans' earlier tokens, 3 + g the prompt of group g, 11 + r request r's own tokens.
All inputs are finite; a program needn't handle non-finite values.
Results may differ from the reference program's by a relative error of at most 0.015.
Values may be sent and summed in bfloat16 or wider, within the bound.
No kernel may reach another device: no remote copies, remote signals or barrier semaphores. Data moves between devices by JAX's collectives and lax.ppermute only.
A program may use at most 192 MiB of HBM per device.

```python
import math
import jax
import jax.numpy as jnp
import numpy as np
from jax import lax

D = 4096
HEADS = 16
HD = 128
ROT = 32
SPANS = 3
GROUPS = 8
PTOK_DEV = 256
PTOK = 8192
REQS = 64
POOL = 25600
OWNERS = 75


def draw_slot_owner(key, part):
    page_count = POOL // 16
    base = jax.random.fold_in(key, 11)
    owner_key, fill_key = jax.random.split(base)
    raw_owner = jax.random.randint(owner_key, (page_count,), 0, 2 * OWNERS)
    page_owner = jnp.where(raw_owner < OWNERS, raw_owner, raw_owner % (SPANS + GROUPS))
    page_owner = jnp.sort(page_owner)
    page_owner = page_owner.at[-1].set(OWNERS - 1)
    run_end = jnp.concatenate([page_owner[1:] != page_owner[:-1], jnp.ones((1,), dtype=bool)])
    page_fill = jnp.where(run_end, jax.random.randint(fill_key, (page_count,), 1, 16), 16)
    page_fill = page_fill.at[-1].set(8)
    slot_index = jnp.arange(16)
    owners = jnp.where(slot_index[None, :] < page_fill[:, None], page_owner[:, None], -1)
    return owners.reshape(POOL).astype(jnp.int32)


def draw_kv_cache(key, part):
    base = jax.random.fold_in(key, 23)
    key_draw, value_draw = jax.random.split(base, 2)
    shape = (POOL, HEADS, HD)
    cached_keys = jnp.clip(jax.random.normal(key_draw, shape, jnp.float32), -5.0, 5.0)
    cached_values = jnp.clip(jax.random.normal(value_draw, shape, jnp.float32), -4.0, 4.0)
    return jnp.stack([cached_keys, cached_values]).astype(jnp.bfloat16)


def draw_prefill_x(key, part):
    base = jax.random.fold_in(key, 31)
    token_draw, region_draw = jax.random.split(base)
    region_count = PTOK // PTOK_DEV + 1
    token_index = jnp.arange(PTOK)
    region_index = (token_index + PTOK_DEV // 2) // PTOK_DEV
    own_part = jnp.clip(jax.random.normal(token_draw, (PTOK, D), jnp.float32), -4.0, 4.0)
    shared_part = jnp.clip(1.2 * jax.random.normal(region_draw, (region_count, D), jnp.float32), -4.0, 4.0)
    return (own_part + shared_part[region_index]).astype(jnp.bfloat16)


def plant(values, key, smallest, largest):
    shape = values.shape
    place = [jax.random.randint(jax.random.fold_in(key, axis), (), 0, shape[axis]) for axis in range(len(shape))]
    values = values.at[tuple(place)].set(smallest)
    longest = shape.index(max(shape))
    place[longest] = (place[longest] + 1) % shape[longest]
    return values.at[tuple(place)].set(largest)


def shard_levels(stream_key, extent, shards, low, largest):
    loudness, own = 1.0, jax.random.fold_in(stream_key, 6)
    for position, blocks in shards:
        heights = jnp.exp(jax.random.uniform(jax.random.fold_in(own, position), (blocks,), jnp.float32, low / len(shards), largest / len(shards)))
        loudness = loudness * jnp.repeat(heights, extent[position] // blocks).reshape([-1 if axis == position else 1 for axis in range(len(extent))])
    return loudness


def length_profile(amount, total, bound, slope):
    portions = [(1 << 20) // math.isqrt(standing ** slope) + 1 for standing in range(2, amount + 1)]
    rest, holding = total - bound - (amount - 1), [1] * (amount - 1)
    while rest > 0:
        movable = [i for i in range(amount - 1) if holding[i] < bound]
        mass, budget = sum([portions[i] for i in movable]), rest
        for i in movable:
            addition = min(bound - holding[i], max(1, budget * portions[i] // mass), rest)
            holding[i] = holding[i] + addition
            rest = rest - addition
    return np.array([bound] + holding)


def ragged_sizes(own_key, count, total, most, skew):
    if count == 2:
        one = jax.random.randint(own_key, (), max(1, total - most), min(most, total - 1) + 1)
        return jnp.stack([one, total - one])
    lengths = jnp.asarray(length_profile(count, total, most, skew), jnp.int32)
    couples = (count - 1) // 2
    donor, receiver = lengths[1:1 + 2 * couples:2], lengths[2:2 + 2 * couples:2]
    slack = jnp.minimum(donor - 1, most - receiver)
    passed = jax.random.randint(jax.random.fold_in(own_key, 1), (couples,), 0, 1 << 20) % (slack + 1)
    lengths = lengths.at[1:1 + 2 * couples:2].set(donor - passed).at[2:2 + 2 * couples:2].set(receiver + passed)
    return lengths[jax.random.permutation(jax.random.fold_in(own_key, 2), count)]


def centred(key, shape, scale, bound, cuts=(), held_as=jnp.bfloat16):
    loudness = shard_levels(key, shape, cuts, -0.22, 0.18) if cuts else 1.0
    values = jax.random.normal(key, shape, jnp.float32) * scale * loudness
    return jnp.minimum(jnp.maximum(values, -bound), bound).astype(held_as)


def setup_inputs(seed: int = 0) -> dict:
    key_list = jax.random.split(jax.random.key(seed), 13)
    return {
        "prefill_x": draw_prefill_x(jax.random.fold_in(key_list[12], 71), 0),
        "decode_x": centred(key_list[1], (REQS, D), 1.0, 6.0, ((0, 32),)),
        "ln_gain": jnp.clip(1.0 + 0.18 * jax.random.normal(key_list[2], (D,), jnp.float32), 0.1, 1.9),
        "ln_bias": centred(key_list[3], (D,), 0.3, 1.75, (), jnp.float32),
        "wqkv": centred(key_list[4], (D, HEADS, 3, HD), D ** -0.5, 0.09375, ((1, 8),)),
        "qkv_bias": centred(key_list[5], (HEADS, 3, HD), 0.5, 3.0, ((0, 8),), jnp.float32),
        "dense_w": centred(key_list[6], (HEADS, HD, D), (HEADS * HD) ** -0.5, 0.125, ((0, 8),)),
        "dense_bias": centred(key_list[7], (D,), 0.5, 3.0, ((0, 8),), jnp.float32),
        "kv_cache": draw_kv_cache(jax.random.fold_in(key_list[12], 71), 0),
        "slot_owner": draw_slot_owner(jax.random.fold_in(key_list[12], 71), 0),
        "group_of": plant(jax.random.randint(key_list[10], (REQS,), 0, GROUPS), jax.random.fold_in(key_list[10], 1), 0, GROUPS - 1).astype(jnp.int32),
        "span_lens": ragged_sizes(key_list[11], SPANS, PTOK, PTOK // 2, 2).astype(jnp.int32),
    }


NEG_FILL = -1e+30

def layer_norm(inputs, ln_gain, ln_bias):
    values = inputs.astype(jnp.float32)
    center = lax.optimization_barrier(jnp.mean(values, axis=-1, keepdims=True))
    spread = lax.optimization_barrier(jnp.mean(jnp.square(values - center), axis=-1, keepdims=True))
    return ((values - center) * lax.rsqrt(spread + 1e-05) * ln_gain + ln_bias).astype(jnp.bfloat16)

def rotary(vectors, positions):
    half_rot = ROT // 2
    exponent = jnp.arange(half_rot, dtype=jnp.float32) * (-2.0 / ROT)
    inverse = jnp.power(jnp.float32(10000.0), exponent)
    angles = positions.astype(jnp.float32)[:, None] * inverse[None, :]
    cosine_table = jnp.cos(angles)[:, None, :]
    sine_table = jnp.sin(angles)[:, None, :]
    first_part = vectors[..., :half_rot]
    second_part = vectors[..., half_rot:ROT]
    remainder = vectors[..., ROT:]
    return jnp.concatenate([first_part * cosine_table - second_part * sine_table, second_part * cosine_table + first_part * sine_table, remainder], axis=-1)

def span_layout(span_lens, counts, total_tokens):
    token_index = jnp.arange(total_tokens, dtype=jnp.int32)
    span_ends = jnp.cumsum(span_lens).astype(jnp.int32)
    span_starts = (span_ends - span_lens).astype(jnp.int32)
    span_ids = lax.optimization_barrier(jnp.sum((token_index[:, None] >= span_ends[None, :SPANS - 1]).astype(jnp.int32), axis=1)).astype(jnp.int32)
    selector = span_ids[:, None] == jnp.arange(SPANS, dtype=jnp.int32)[None, :]
    start_of = lax.optimization_barrier(jnp.sum(jnp.where(selector, span_starts[None, :], 0), axis=1)).astype(jnp.int32)
    cached_of = lax.optimization_barrier(jnp.sum(jnp.where(selector, counts[None, :SPANS], 0), axis=1)).astype(jnp.int32)
    return (span_ids, (cached_of + token_index - start_of).astype(jnp.int32))

def decode_layout(group_of, counts):
    groups_hit = group_of[:, None] == jnp.arange(GROUPS, dtype=jnp.int32)[None, :]
    prompt_len = lax.optimization_barrier(jnp.sum(jnp.where(groups_hit, counts[None, SPANS:SPANS + GROUPS], 0), axis=1)).astype(jnp.int32)
    return (prompt_len + counts[SPANS + GROUPS:]).astype(jnp.int32)

def reference(prefill_x, decode_x, ln_gain, ln_bias, wqkv, qkv_bias, dense_w, dense_bias, kv_cache, slot_owner, group_of, span_lens):
    owner_ids = jnp.arange(OWNERS, dtype=jnp.int32)
    counts = lax.optimization_barrier(jnp.sum((slot_owner[:, None] == owner_ids[None, :]).astype(jnp.int32), axis=0)).astype(jnp.int32)
    span_ids, span_pos = span_layout(span_lens, counts, PTOK)
    own_labels = (SPANS + GROUPS + jnp.arange(REQS, dtype=jnp.int32)).astype(jnp.int32)
    decode_pos = decode_layout(group_of, counts)
    inputs = jnp.concatenate([prefill_x, decode_x], axis=0)
    normed = layer_norm(inputs, ln_gain, ln_bias)
    projected = jnp.dot(normed, wqkv.reshape(D, HEADS * 3 * HD), preferred_element_type=jnp.float32)
    projected = projected.reshape(-1, HEADS, 3, HD) + qkv_bias
    positions = jnp.concatenate([span_pos, decode_pos], axis=0)
    queries = rotary(projected[:, :, 0], positions).astype(jnp.bfloat16)
    new_keys = rotary(projected[:, :, 1], positions).astype(jnp.bfloat16)
    new_values = projected[:, :, 2].astype(jnp.bfloat16)
    first_label = jnp.concatenate([span_ids, (SPANS + group_of).astype(jnp.int32)], axis=0)
    second_label = jnp.concatenate([span_ids, own_labels], axis=0)
    key_labels = jnp.concatenate([slot_owner, second_label], axis=0)
    key_pos = jnp.concatenate([jnp.full((POOL,), -1, jnp.int32), positions], axis=0)
    visible = ((key_labels[None, :] == first_label[:, None]) | (key_labels[None, :] == second_label[:, None])) & (key_pos[None, :] <= positions[:, None])
    all_keys = jnp.transpose(jnp.concatenate([kv_cache[0], new_keys], axis=0), (1, 0, 2))
    all_values = jnp.transpose(jnp.concatenate([kv_cache[1], new_values], axis=0), (1, 0, 2))
    query_heads = jnp.transpose(queries, (1, 0, 2))

    def one_head(operands):
        head_query, head_keys, head_values = operands
        scores = jnp.dot(head_query, head_keys.T, preferred_element_type=jnp.float32) / math.sqrt(HD)
        scores = jnp.where(visible, scores, NEG_FILL)
        row_top = lax.optimization_barrier(jnp.max(scores, axis=1, keepdims=True))
        weights = jnp.exp(scores - row_top)
        totals = lax.optimization_barrier(jnp.sum(weights, axis=1, keepdims=True))
        weighted = jnp.dot(weights.astype(jnp.bfloat16), head_values, preferred_element_type=jnp.float32)
        return (weighted / totals).astype(jnp.bfloat16)
    attended = lax.map(one_head, (query_heads, all_keys, all_values))
    flat = jnp.transpose(attended, (1, 0, 2)).reshape(-1, HEADS * HD)
    mixed_out = jnp.dot(flat, dense_w.reshape(HEADS * HD, D), preferred_element_type=jnp.float32) + dense_bias
    mixed_out = mixed_out.astype(jnp.bfloat16)
    return (mixed_out[:PTOK], mixed_out[PTOK:])
```

```python
import functools
import math

import jax
import jax.numpy as jnp
from jax import lax
from jax.experimental import pallas as pl
from jax.experimental.pallas import tpu as pltpu
from jax.sharding import Mesh
from jax.sharding import PartitionSpec as P

ROT = 32
SPANS = 3
GROUPS = 8
X, Z, Y, C = 4, 8, 4, 2
HEAD = 128
NEG = -1e30
LOW = -1e29
SCALE = math.log2(math.e) / math.sqrt(HEAD)
BF = jnp.bfloat16
F32 = jnp.float32
I32 = jnp.int32


def shift(value, axis, size, step):
    return lax.ppermute(value, axis, [(i, (i + step) % size) for i in range(size)])


def layer_norm(inputs, ln_gain, ln_bias):
    values = inputs.astype(F32)
    center = jnp.mean(values, axis=-1, keepdims=True)
    spread = jnp.mean(jnp.square(values - center), axis=-1, keepdims=True)
    return ((values - center) * lax.rsqrt(spread + 1e-05) * ln_gain + ln_bias).astype(BF)


def rotary(vectors, cosine, sine):
    half = ROT // 2
    first, second, rest = vectors[..., :half], vectors[..., half:ROT], vectors[..., ROT:]
    return jnp.concatenate(
        [first * cosine - second * sine, second * cosine + first * sine, rest], axis=-1
    )


def pieces(value, count):
    out = []
    for _ in range(count):
        part = value.astype(BF).astype(F32)
        out.append(part)
        value = value - part
    return out


def nt_dot(a, b):
    return lax.dot_general(a, b, (((1,), (1,)), ((), ())), preferred_element_type=F32)


def attend_kernel(rows, slots, fresh, chunks, sc, *refs):
    nq = Z
    q_refs, refs = refs[:nq], refs[nq:]
    kv_refs, refs = refs[:fresh], refs[fresh:]
    cache_refs, refs = refs[:5], refs[5:]
    out_refs, refs = refs[:nq], refs[nq:]
    qs, kvs, cs, wide, ck, msg, m_s, l_s, acc_s, q_sem, kv_sem, c_sem, o_sem = refs
    x, z = sc[0], sc[1]
    starts = (0, sc[2], sc[3])
    ends = (sc[2], sc[3], X * Z * rows)
    lows = (sc[4], sc[6], sc[8])
    highs = (sc[5], sc[7], sc[9])

    for t in range(2):
        for where_x, ref in ((0, cache_refs[0]), (1, cache_refs[1]), (3, cache_refs[2])):
            @pl.when(x == where_x)
            def _():
                pltpu.make_async_copy(ref.at[t], cs.at[t], c_sem.at[t]).start()

        @pl.when(x == 2)
        def _():
            pltpu.make_async_copy(cache_refs[3 + t], cs.at[t], c_sem.at[t]).start()

    for s in range(nq):
        pltpu.make_async_copy(q_refs[s], qs.at[s], q_sem.at[s]).start()
    for r in range(fresh):
        pltpu.make_async_copy(kv_refs[r], kvs.at[r], kv_sem.at[r]).start()

    for t in range(2):
        pltpu.make_async_copy(cache_refs[3 + t], cs.at[t], c_sem.at[t]).wait()
        wide[...] = cs[t].astype(F32)
        for h in range(2):
            ck[t, h] = wide[pl.ds(h, slots, stride=2), :].astype(BF)
    for r in range(fresh):
        pltpu.make_async_copy(kv_refs[r], kvs.at[r], kv_sem.at[r]).wait()

    def block(s, carry):
        pltpu.make_async_copy(q_refs[0], qs.at[s], q_sem.at[s]).wait()
        zq = lax.rem(z - s + Z, Z)
        base = (x * Z + zq) * rows
        qt = base + lax.broadcasted_iota(I32, (rows, 1), 0)

        def pick(a):
            return jnp.where(qt >= starts[2], a[2], jnp.where(qt >= starts[1], a[1], a[0]))

        start_q, lo_q, hi_q = pick(starts), pick(lows), pick(highs)
        first_start = jnp.where(
            base >= starts[2], starts[2], jnp.where(base >= starts[1], starts[1], 0)
        )
        m_s[...] = jnp.full_like(m_s, LOW)
        l_s[...] = jnp.zeros_like(l_s)
        acc_s[...] = jnp.zeros_like(acc_s)

        def tile(keys, values, mask):
            for h in range(2):
                scores = jnp.where(mask, nt_dot(qs[s, h], keys(h)), NEG)
                m_old = m_s[h]
                m_new = jnp.maximum(m_old, jnp.max(scores, axis=1, keepdims=True))
                alpha = jnp.exp2((m_old - m_new) * SCALE)
                p = jnp.exp2((scores - m_new[:, :1]) * SCALE)
                l_s[h] = alpha * l_s[h] + jnp.sum(p, axis=1, keepdims=True)
                acc_s[h] = alpha * acc_s[h] + jnp.dot(
                    p.astype(BF), values(h), preferred_element_type=F32
                )
                m_s[h] = m_new

        for r in range(fresh):
            kb = ((x - r) * Z + z) * rows

            @pl.when((x >= r) & (kb <= base + rows - 1) & (kb + rows > first_start))
            def _():
                kt = kb + lax.broadcasted_iota(I32, (1, rows), 1)
                tile(
                    lambda h: kvs[r, 0, h],
                    lambda h: kvs[r, 1, h],
                    (kt >= start_q) & (kt <= qt),
                )

        for a, n in chunks:
            need = False
            for c in range(SPANS):
                here = (base < ends[c]) & (base + rows > starts[c])
                need = need | (
                    here & (lows[c] < a + n) & (highs[c] > a) & (highs[c] > lows[c])
                )

            @pl.when(need)
            def _():
                kidx = a + lax.broadcasted_iota(I32, (1, n), 1)
                tile(
                    lambda h: ck[0, h, pl.ds(a, n), :],
                    lambda h: ck[1, h, pl.ds(a, n), :],
                    (kidx >= lo_q) & (kidx < hi_q),
                )

        lane = lax.broadcasted_iota(I32, (rows, HEAD), 1)
        stats = jnp.zeros((rows, HEAD), F32)
        for h in range(2):
            total = l_s[h]
            inverse = 1.0 / jnp.where(total > 0, total, 1.0)
            msg[s, pl.ds(0, rows), pl.ds(h * HEAD, HEAD)] = (acc_s[h] * inverse).astype(BF)
            for k, part in enumerate(pieces(m_s[h], 3) + pieces(total, 2)):
                stats = jnp.where(lane == 5 * h + k, part, stats)
        msg[s, pl.ds(rows, 16), :] = jnp.transpose(stats)[:16].astype(BF)
        for k in range(nq):
            @pl.when(s == k)
            def _():
                pltpu.make_async_copy(msg.at[k], out_refs[k], o_sem.at[k]).start()
        return carry

    lax.fori_loop(0, nq, block, 0)
    for s in range(nq):
        pltpu.make_async_copy(msg.at[s], out_refs[s], o_sem.at[s]).wait()


def attend(sc, queries, fresh, caches):
    rows = queries[0].shape[1]
    slots = caches[0].shape[1] // 2
    chunks, at = [], 0
    while at < slots:
        size = 256 if slots - at >= 512 else slots - at
        chunks.append((at, size))
        at += size
    any_spec = pl.BlockSpec(memory_space=pl.ANY)
    operands = (*queries, *fresh, *caches)
    nf = len(fresh)
    return pl.pallas_call(
        functools.partial(attend_kernel, rows, slots, nf, tuple(chunks)),
        out_shape=[jax.ShapeDtypeStruct((rows + 16, 2 * HEAD), BF)] * Z,
        in_specs=[pl.BlockSpec(memory_space=pltpu.SMEM)] + [any_spec] * len(operands),
        out_specs=[any_spec] * Z,
        scratch_shapes=[
            pltpu.VMEM((Z, 2, rows, HEAD), BF),
            pltpu.VMEM((max(nf, 1), 2, 2, rows, HEAD), BF),
            pltpu.VMEM((2, 2 * slots, HEAD), BF),
            pltpu.VMEM((2 * slots, HEAD), F32),
            pltpu.VMEM((2, 2, slots, HEAD), BF),
            pltpu.VMEM((Z, rows + 16, 2 * HEAD), BF),
            pltpu.VMEM((2, rows, HEAD), F32),
            pltpu.VMEM((2, rows, HEAD), F32),
            pltpu.VMEM((2, rows, HEAD), F32),
            pltpu.SemaphoreType.DMA((Z,)),
            pltpu.SemaphoreType.DMA((max(nf, 1),)),
            pltpu.SemaphoreType.DMA((2,)),
            pltpu.SemaphoreType.DMA((Z,)),
        ],
        compiler_params=pltpu.CompilerParams(vmem_limit_bytes=40 << 20),
        cost_estimate=pl.CostEstimate(
            flops=6_000_000_000, bytes_accessed=8_000_000, transcendentals=8_000_000
        ),
        name="attend",
    )(sc, *operands)


def decode_kernel(q_ref, info_ref, owner_ref, kv_ref, out_ref):
    owner = owner_ref[...]
    first, second, head = info_ref[:, 0:1], info_ref[:, 1:2], info_ref[:, 2:3]
    parity = lax.broadcasted_iota(I32, owner.shape, 1) & 1
    mask = ((owner == first) | (owner == second)) & (parity == head)
    scores = jnp.where(mask, nt_dot(q_ref[...], kv_ref[0]), NEG)
    top = jnp.maximum(jnp.max(scores, axis=1, keepdims=True), LOW)
    p = jnp.exp2((scores - top) * SCALE)
    out_ref[:, :HEAD] = jnp.dot(p.astype(BF), kv_ref[1], preferred_element_type=F32)
    lane = lax.broadcasted_iota(I32, (out_ref.shape[0], HEAD), 1)
    total = jnp.sum(p, axis=1, keepdims=True)
    out_ref[:, HEAD:] = jnp.where(lane == 0, top, jnp.where(lane == 1, total, 0.0))


def decode_attend(queries, info, owner, kv):
    count = queries.shape[0]
    return pl.pallas_call(
        decode_kernel,
        out_shape=jax.ShapeDtypeStruct((count, 2 * HEAD), F32),
        cost_estimate=pl.CostEstimate(
            flops=110_000_000, bytes_accessed=1_000_000, transcendentals=210_000
        ),
        name="decode_attend",
    )(queries, info, owner, kv)


def merge_parts(parts):
    parts = jnp.stack(parts)
    tops = parts[..., HEAD : HEAD + 1]
    top = jnp.max(tops, axis=0)
    scaled = parts * jnp.exp2((tops - top) * SCALE)
    total = jnp.sum(scaled, axis=0)
    lane = lax.broadcasted_iota(I32, total.shape, total.ndim - 1)
    return jnp.where(lane == HEAD, top, total)


def combine_kernel(rows, *refs):
    msgs, out_ref = refs[:-1], refs[-1]
    n = len(msgs)
    stats = [m[pl.ds(rows, 16), :].astype(F32) for m in msgs]
    weights = []
    for h in range(2):
        tops = [s[5 * h : 5 * h + 1] + s[5 * h + 1 : 5 * h + 2] + s[5 * h + 2 : 5 * h + 3] for s in stats]
        totals = [s[5 * h + 3 : 5 * h + 4] + s[5 * h + 4 : 5 * h + 5] for s in stats]
        top = functools.reduce(jnp.maximum, tops)
        shares = [t * jnp.exp2((m - top) * SCALE) for m, t in zip(tops, totals)]
        inverse = 1.0 / functools.reduce(jnp.add, shares)
        weights += [s * inverse for s in shares]
    table = jnp.concatenate(weights + [jnp.zeros((HEAD - 2 * n, rows), F32)], axis=0)
    columns = jnp.transpose(table)
    for h in range(2):
        total = jnp.zeros((rows, HEAD), F32)
        for i, m in enumerate(msgs):
            k = h * n + i
            total += columns[:, k : k + 1] * m[pl.ds(0, rows), pl.ds(h * HEAD, HEAD)].astype(F32)
        out_ref[:, h * HEAD : (h + 1) * HEAD] = total.astype(BF)


def combine(msgs):
    rows = msgs[0].shape[0] - 16
    return pl.pallas_call(
        functools.partial(combine_kernel, rows),
        out_shape=jax.ShapeDtypeStruct((rows, 2 * HEAD), BF),
        cost_estimate=pl.CostEstimate(
            flops=2_000_000, bytes_accessed=1_300_000, transcendentals=10_000
        ),
        name="combine",
    )(*msgs)


def project_kernel(sc, *refs):
    parts, w_ref, bias_ref, out_ref = refs[:Y], refs[Y], refs[Y + 1], refs[Y + 2]
    y = sc[0]
    total = jnp.zeros(out_ref.shape, F32)
    for r in range(Y):
        yy = lax.rem(y - r + Y, Y)
        for c in range(C):
            total += jnp.dot(parts[r][c], w_ref[yy * C + c], preferred_element_type=F32)
    out_ref[...] = (total + bias_ref[...]).astype(BF)


def project(sc, parts, w, bias):
    rows, cols = parts[0].shape[1], w.shape[2]
    vmem = pl.BlockSpec(memory_space=pltpu.VMEM)
    return pl.pallas_call(
        project_kernel,
        out_shape=jax.ShapeDtypeStruct((rows, cols), BF),
        in_specs=[pl.BlockSpec(memory_space=pltpu.SMEM)] + [vmem] * (Y + 2),
        out_specs=vmem,
        cost_estimate=pl.CostEstimate(
            flops=550_000_000, bytes_accessed=3_500_000, transcendentals=0
        ),
        name="project",
    )(sc, *parts, w, bias)


def merge_messages(a, b, rows):
    def parse(m):
        stats = m[rows:].astype(F32)
        out = []
        for h in range(2):
            s = stats[5 * h : 5 * h + 5]
            out.append((s[0] + s[1] + s[2], s[3] + s[4]))
        return out

    results, stat_rows = [], []
    for h, ((ma, la), (mb, lb)) in enumerate(zip(parse(a), parse(b))):
        top = jnp.maximum(ma, mb)
        wa = la * jnp.exp2((ma - top) * SCALE)
        wb = lb * jnp.exp2((mb - top) * SCALE)
        total = wa + wb
        inverse = 1.0 / jnp.where(total > 0, total, 1.0)
        part = slice(h * HEAD, (h + 1) * HEAD)
        results.append(
            (wa * inverse)[:, None] * a[:rows, part].astype(F32)
            + (wb * inverse)[:, None] * b[:rows, part].astype(F32)
        )
        for value, count in ((top, 3), (total, 2)):
            for _ in range(count):
                piece = lax.reduce_precision(value, 8, 7)
                stat_rows.append(piece)
                value = value - piece
    stat_rows += [jnp.zeros_like(stat_rows[0])] * 6
    return jnp.concatenate(
        [jnp.concatenate(results, axis=1).astype(BF), jnp.stack(stat_rows).astype(BF)]
    )


def on_device(
    prefill_x,
    decode_x,
    ln_gain,
    ln_bias,
    wqkv,
    qkv_bias,
    dense_w,
    dense_bias,
    kv_cache,
    slot_owner,
    group_of,
    span_lens,
):
    x, z = lax.axis_index("x"), lax.axis_index("z")
    y = lax.axis_index("y")
    rows, dec = prefill_x.shape[0], decode_x.shape[0]
    slots = slot_owner.shape[0]
    requests = group_of.shape[0]
    owners = SPANS + GROUPS + requests
    cache = kv_cache.reshape(2, 2 * slots, HEAD)

    cache_1 = lax.ppermute(cache, "x", [(0, 1)])
    cache_3 = lax.ppermute(cache, "x", [(0, 3)])
    cache_2k = lax.ppermute(cache_1[0], "x", [(1, 2)])
    cache_2v = lax.ppermute(cache_3[1], "x", [(3, 2)])

    width = dense_w.shape[2]
    w_out = dense_w.reshape(2 * HEAD, Y * C, width // (Y * C)).transpose(1, 0, 2)
    w_out = lax.all_to_all(w_out, ("y", "core"), 0, 0)

    owner_ids = jnp.arange(HEAD, dtype=I32)
    hits = (slot_owner[:, None] == owner_ids[None, :]) & (owner_ids < owners)[None, :]
    local = jnp.sum(hits.astype(F32), axis=0)
    begin = jnp.min(
        jnp.where(hits[:, :SPANS], jnp.arange(slots, dtype=I32)[:, None], slots), axis=0
    ).astype(F32)
    extra = jnp.where(x > 0, jnp.sum(local[:SPANS]), 0.0)
    vector = jnp.where(owner_ids == HEAD - 1, extra, local)
    over_z = vector
    for s in range(1, Z):
        over_z = over_z + shift(vector, "z", Z, s)
    at_row = jnp.where(x == 0, 1.0, 0.0) * jnp.concatenate([begin, begin + local[:SPANS]])
    pair = jnp.concatenate([over_z, at_row, jnp.zeros((HEAD - 2 * SPANS,), F32)])
    total = pair
    for r in range(1, X):
        total = total + shift(pair, "x", X, r)
    counts = total[:owners].astype(I32)
    more = total[HEAD - 1] > 0
    ranges = total[HEAD : HEAD + 2 * SPANS].astype(I32)

    index = x * Z + z
    ends = jnp.cumsum(span_lens)
    begins = ends - span_lens
    token = index * rows + jnp.arange(rows, dtype=I32)
    span = jnp.sum((token[:, None] >= ends[None, : SPANS - 1]).astype(I32), axis=1)
    chosen = span[:, None] == jnp.arange(SPANS, dtype=I32)[None, :]
    span_pos = token + jnp.sum(jnp.where(chosen, (counts[:SPANS] - begins)[None, :], 0), axis=1)
    request = index * dec + jnp.arange(dec, dtype=I32)
    my_group = jnp.sum(
        jnp.where(request[:, None] == jnp.arange(requests, dtype=I32), group_of[None, :], 0), axis=1
    )
    all_owner = jnp.arange(owners, dtype=I32)
    decode_pos = jnp.sum(
        jnp.where(
            (all_owner == SPANS + my_group[:, None])
            | (all_owner == SPANS + GROUPS + request[:, None]),
            counts[None, :],
            0,
        ),
        axis=1,
    )
    positions = jnp.concatenate([span_pos, decode_pos])

    normed = layer_norm(jnp.concatenate([prefill_x, decode_x], axis=0), ln_gain, ln_bias)
    projected = jnp.einsum("td,dhje->hjte", normed, wqkv, preferred_element_type=F32)
    projected = projected + qkv_bias[:, :, None, :]
    exponent = jnp.arange(ROT // 2, dtype=F32) * (-2.0 / ROT)
    angles = positions.astype(F32)[:, None] * jnp.power(F32(10000.0), exponent)[None, :]
    cosine, sine = jnp.cos(angles), jnp.sin(angles)
    queries = rotary(projected[:, 0], cosine, sine).astype(BF)
    new_keys = rotary(projected[:, 1], cosine, sine).astype(BF)
    new_values = projected[:, 2].astype(BF)
    my_q, dec_q = queries[:, :rows], queries[:, rows:]
    fresh = jnp.stack([new_keys[:, :rows], new_values[:, :rows]])

    own = dec_q.reshape(2 * dec, HEAD)
    over_x = jnp.concatenate([own] + [shift(own, "x", X, r) for r in range(1, X)])
    all_q = [my_q] + [shift(my_q, "z", Z, s) for s in range(1, Z)]
    all_kv = [fresh] + [
        lax.ppermute(fresh, "x", [(i, i + r) for i in range(X - r)]) for r in (1, 2)
    ]
    everyone = jnp.concatenate([over_x] + [shift(over_x, "z", Z, s) for s in range(1, Z)])

    row = jnp.arange(Z * X * 2 * dec, dtype=I32)
    from_s, from_r = row // (X * 2 * dec), (row // (2 * dec)) % X
    row_head, row_i = (row // dec) % 2, row % dec
    row_req = (((x - from_r + X) % X) * Z + (z - from_s + Z) % Z) * dec + row_i
    row_group = jnp.sum(
        jnp.where(row_req[:, None] == jnp.arange(requests, dtype=I32), group_of[None, :], 0), axis=1
    )
    info = jnp.stack([SPANS + row_group, SPANS + GROUPS + row_req, row_head], axis=1)
    parts = decode_attend(everyone, info, jnp.repeat(slot_owner, 2)[None, :], cache)
    parts = parts.reshape(Z, X, 2 * dec, 2 * HEAD)
    part_x = merge_parts(
        [parts[:, 0]] + [shift(parts[:, r], "x", X, X - r) for r in range(1, X)]
    )
    back = [part_x[0]] + [shift(part_x[s], "z", Z, Z - s) for s in range(1, Z)]
    dec_k = new_keys[:, rows:].reshape(2 * dec, HEAD)
    dec_v = new_values[:, rows:].reshape(2 * dec, HEAD).astype(F32)
    self_score = jnp.sum(own.astype(F32) * dec_k.astype(F32), axis=1, keepdims=True)
    self_part = jnp.concatenate(
        [dec_v, self_score, jnp.ones_like(self_score), jnp.zeros((2 * dec, HEAD - 2), F32)], axis=1
    )
    final = merge_parts(back + [self_part])
    dec_att = (final[:, :HEAD] / final[:, HEAD + 1 : HEAD + 2]).astype(BF)
    dec_att = dec_att.reshape(2, dec, HEAD).transpose(1, 0, 2).reshape(dec, 2 * HEAD)

    def scalars(bounds):
        return jnp.concatenate([jnp.stack([x, z]), ends[: SPANS - 1], bounds]).astype(I32)

    def interleave(values):
        return jnp.stack([values[:SPANS], values[SPANS:]], axis=1).reshape(-1)

    sc = scalars(interleave(ranges))
    caches = (cache, cache_1, cache_3, cache_2k, cache_2v)

    def common(all_q, all_kv, caches, cache):
        return tuple(attend(sc, all_q, all_kv, caches))

    def general(all_q, all_kv, caches, cache):
        def turn(i, state):
            msgs, held, bounds, row_of = state
            mine = jnp.where(row_of > 0, bounds, jnp.zeros_like(bounds))
            five = (held, held, held, held[0], held[1])
            found = attend(scalars(interleave(mine)), all_q, [], five)
            msgs = tuple(merge_messages(a, b, rows) for a, b in zip(msgs, found))
            return (
                msgs,
                shift(held, "x", X, 1),
                shift(bounds, "x", X, 1),
                shift(row_of, "x", X, 1),
            )

        msgs = tuple(attend(sc, all_q, all_kv, caches))
        bounds = jnp.concatenate([begin, begin + local[:SPANS]]).astype(I32)
        return lax.fori_loop(0, X, turn, (msgs, cache, bounds, x))[0]

    msgs = lax.cond(more, general, common, tuple(all_q), tuple(all_kv), caches, cache)
    home = [msgs[0]] + [shift(msgs[s], "z", Z, Z - s) for s in range(1, Z)]
    attended = jnp.concatenate([combine(home), dec_att], axis=0)

    both = lax.all_gather(attended, "core")
    gathered = [both] + [shift(both, "y", Y, r) for r in range(1, Y)]
    out = project(y[None].astype(I32), gathered, w_out, dense_bias[None, :])
    return out[:rows], out[rows:]


def solution(mesh):
    mesh = Mesh(mesh.devices.reshape(X, Z, Y, C), ("x", "z", "y", "core"))
    seq, tensor = ("x", "z"), ("y", "core")
    in_specs = (
        P(seq, None),
        P(seq, None),
        P(),
        P(),
        P(None, tensor, None, None),
        P(tensor, None, None),
        P(tensor, None, None),
        P(tensor),
        P(None, seq, tensor, None),
        P(seq),
        P(),
        P(),
    )
    out_specs = (P(seq, tensor), P(seq, tensor))
    return jax.shard_map(
        on_device, mesh=mesh, in_specs=in_specs, out_specs=out_specs, check_vma=False
    )
```

```python
import functools
import math

import jax
import jax.numpy as jnp
from jax import lax
from jax.experimental import pallas as pl
from jax.experimental.pallas import tpu as pltpu
from jax.sharding import Mesh
from jax.sharding import PartitionSpec as P


X, Z, Y, C = 4, 8, 4, 2
SPANS, GROUPS, ROT = 3, 8, 32
HEAD = 128
NEG = -1e30
LOW = -1e29
SCALE = math.log2(math.e) / math.sqrt(HEAD)
BF, F32, I32 = jnp.bfloat16, jnp.float32, jnp.int32
TILE = 256

def pieces(value, count):
    out = []
    for _ in range(count):
        part = value.astype(BF).astype(F32)
        out.append(part)
        value = value - part
    return out


def nt_dot(a, b):
    return lax.dot_general(a, b, (((1,), (1,)), ((), ())), preferred_element_type=F32)


def turned(values, cosine, sine):
    lane = lax.broadcasted_iota(I32, values.shape, 1)
    half = ROT // 2
    partner = jnp.where(
        lane < half, pltpu.roll(values, HEAD - half, 1), pltpu.roll(values, half, 1)
    )
    return values * cosine + partner * sine


def attend_kernel(rows, slots, fresh, sc, turn_ref, dec_ref, *refs):
    nq = Z
    q_refs, refs = refs[:nq], refs[nq:]
    kv_refs, refs = refs[:fresh], refs[fresh:]
    cache_refs, refs = refs[:5], refs[5:]
    out_refs, refs = refs[:nq], refs[nq:]
    qs, qx, kk, vv, cs, wide, msg, m_s, acc_s, q_sem, k_sem, v_sem, c_sem, o_sem = refs
    x, z = sc[0], sc[1]
    starts = (0, sc[2], sc[3])
    ends = (sc[2], sc[3], X * Z * rows)
    lows = (sc[4], sc[6], sc[8])
    highs = (sc[5], sc[7], sc[9])
    old = fresh * rows

    for t in range(2):
        for where_x, ref in ((0, cache_refs[0]), (1, cache_refs[1]), (3, cache_refs[2])):
            @pl.when(x == where_x)
            def _():
                pltpu.make_async_copy(ref.at[t], cs.at[t], c_sem.at[t]).start()

        @pl.when(x == 2)
        def _():
            pltpu.make_async_copy(cache_refs[3 + t], cs.at[t], c_sem.at[t]).start()

    for s in range(nq):
        pltpu.make_async_copy(q_refs[s].at[pl.ds(0, 2 * rows)], qs.at[s], q_sem.at[s]).start()
    k_copies, v_copies = [], []
    for r in range(fresh):
        for h in range(2):
            k_copies.append(
                pltpu.make_async_copy(
                    kv_refs[r].at[0, h], kk.at[h, pl.ds(r * rows, rows)], k_sem.at[2 * r + h]
                )
            )
            v_copies.append(
                pltpu.make_async_copy(
                    kv_refs[r].at[1, h],
                    vv.at[h, pl.ds(r * rows, rows), pl.ds(0, HEAD)],
                    v_sem.at[2 * r + h],
                )
            )
    for c in k_copies + v_copies:
        c.start()
    vv[:, :, HEAD:] = jnp.ones((2, vv.shape[1], HEAD), BF)
    spare = vv.shape[1] - old - slots
    if spare:
        kk[:, pl.ds(old + slots, spare), :] = jnp.zeros((2, spare, HEAD), BF)
        vv[:, pl.ds(old + slots, spare), :HEAD] = jnp.zeros((2, spare, HEAD), BF)

    pltpu.make_async_copy(cache_refs[3], cs.at[0], c_sem.at[0]).wait()
    wide[...] = cs[0].astype(F32)
    for h in range(2):
        kk[h, pl.ds(old, slots), :] = wide[pl.ds(h, slots, stride=2), :].astype(BF)
    pltpu.make_async_copy(cache_refs[4], cs.at[1], c_sem.at[1]).wait()
    wide[...] = cs[1].astype(F32)
    for h in range(2):
        vv[h, pl.ds(old, slots), :HEAD] = wide[pl.ds(h, slots, stride=2), :].astype(BF)
    for c in k_copies + v_copies:
        c.wait()

    def block(s, carry):
        pltpu.make_async_copy(q_refs[0].at[pl.ds(0, 2 * rows)], qs.at[s], q_sem.at[s]).wait()
        zq = lax.rem(z - s + Z, Z)
        base = (x * Z + zq) * rows
        qt = base + lax.broadcasted_iota(I32, (rows, 1), 0)
        second, third = qt >= starts[1], qt >= starts[2]

        def pick(a):
            return jnp.where(third, a[2], jnp.where(second, a[1], a[0]))

        start_q, lo_q, hi_q = pick(starts), pick(lows), pick(highs)
        first_start = jnp.where(
            base >= starts[2], starts[2], jnp.where(base >= starts[1], starts[1], 0)
        )
        last_start = jnp.where(
            base + rows > starts[2],
            starts[2],
            jnp.where(base + rows > starts[1], starts[1], 0),
        )
        cosine = pick([turn_ref[pl.ds(c, 1), :] for c in range(SPANS)])
        sine = pick([turn_ref[pl.ds(4 + c, 1), :] for c in range(SPANS)])
        for h in range(2):
            q = qs[s, pl.ds(h * rows, rows), :]
            qx[0, h] = q
            qx[1, h] = turned(q.astype(F32), cosine, sine).astype(BF)
        m_s[...] = jnp.full_like(m_s, LOW)
        acc_s[...] = jnp.zeros_like(acc_s)
        any_lo, any_hi, all_lo, all_hi = slots, 0, 0, slots
        for c in range(SPANS):
            here = (base < ends[c]) & (base + rows > starts[c])
            some = here & (highs[c] > lows[c])
            any_lo = jnp.where(some, jnp.minimum(any_lo, lows[c]), any_lo)
            any_hi = jnp.where(some, jnp.maximum(any_hi, highs[c]), any_hi)
            all_lo = jnp.where(here, jnp.maximum(all_lo, lows[c]), all_lo)
            all_hi = jnp.where(here, jnp.minimum(all_hi, highs[c]), all_hi)

        def tile(j, carry):
            is_old = j >= fresh
            kb = jnp.where(is_old, (j - fresh) * TILE, ((x - j) * Z + z) * rows)
            need_new = (x >= j) & (kb <= base + rows - 1) & (kb + TILE > first_start)
            full_new = (kb + TILE - 1 <= base) & (kb >= last_start)
            need_old = (kb < any_hi) & (kb + TILE > any_lo)
            full_old = (kb >= all_lo) & (kb + TILE <= all_hi)
            need = jnp.where(is_old, need_old, need_new)
            full = jnp.where(is_old, full_old, full_new)
            which = jnp.where(is_old, 1, 0)
            at = pl.multiple_of(j * TILE, TILE)

            def update(mask):
                all_s = [nt_dot(qx[which, h], kk[h, pl.ds(at, TILE), :]) for h in range(2)]
                if mask is not None:
                    all_s = [jnp.where(mask, s_, NEG) for s_ in all_s]
                tops = [jnp.max(s_, axis=1, keepdims=True) for s_ in all_s]
                ps = []
                for h in range(2):
                    m_old = m_s[h]
                    m_new = jnp.maximum(m_old, tops[h])
                    alpha = jnp.exp2((m_old - m_new) * SCALE)
                    wide_m = jnp.concatenate([m_new] * (TILE // HEAD), axis=1)
                    ps.append((jnp.exp2((all_s[h] - wide_m) * SCALE).astype(BF), alpha))
                    m_s[h] = m_new
                for h in range(2):
                    p, alpha = ps[h]
                    acc_s[h] = jnp.concatenate([alpha, alpha], axis=1) * acc_s[h] + jnp.dot(
                        p, vv[h, pl.ds(at, TILE), :], preferred_element_type=F32
                    )

            @pl.when(need & full)
            def _():
                update(None)

            @pl.when(need & jnp.logical_not(full))
            def _():
                key = kb + lax.broadcasted_iota(I32, (1, TILE), 1)
                low = jnp.where(is_old, lo_q, start_q)
                high = jnp.where(is_old, hi_q - 1, qt)
                update((key >= low) & (key <= high))

            return carry

        lax.fori_loop(0, kk.shape[1] // TILE, tile, 0)

        lane = lax.broadcasted_iota(I32, (rows, HEAD), 1)
        stats = jnp.zeros((rows, HEAD), F32)
        for h in range(2):
            total = acc_s[h, :, HEAD:]
            inverse = 1.0 / jnp.where(total > 0, total, 1.0)
            msg[s, pl.ds(0, rows), pl.ds(h * HEAD, HEAD)] = (acc_s[h, :, :HEAD] * inverse).astype(BF)
            for k, part in enumerate(pieces(m_s[h], 3) + pieces(total, 2)):
                stats = jnp.where(lane == 5 * h + k, part, stats)
        msg[s, pl.ds(rows, 16), :] = jnp.transpose(stats)[:16].astype(BF)
        part = dec_ref[s]
        top, total = part[:, HEAD : HEAD + 1], part[:, HEAD + 1 : HEAD + 2]
        inverse = 1.0 / jnp.where(total > 0, total, 1.0)
        lane = lax.broadcasted_iota(I32, (16, HEAD), 1)
        stats = jnp.zeros((16, HEAD), F32)
        for k, piece in enumerate(pieces(top, 3) + pieces(total, 2)):
            stats = jnp.where(lane == k, piece, stats)
        msg[s, pl.ds(rows + 16, 16), pl.ds(0, HEAD)] = (part[:, :HEAD] * inverse).astype(BF)
        msg[s, pl.ds(rows + 16, 16), pl.ds(HEAD, HEAD)] = stats.astype(BF)
        for k in range(nq):
            @pl.when(s == k)
            def _():
                pltpu.make_async_copy(msg.at[k], out_refs[k], o_sem.at[k]).start()
        return carry

    lax.fori_loop(0, nq, block, 0)
    for s in range(nq):
        pltpu.make_async_copy(msg.at[s], out_refs[s], o_sem.at[s]).wait()


def attend(sc, turn, dec, queries, fresh, caches):
    rows = fresh[0].shape[2] if fresh else TILE
    slots = caches[0].shape[1] // 2
    keys = len(fresh) * rows + -(-slots // TILE) * TILE
    any_spec = pl.BlockSpec(memory_space=pl.ANY)
    operands = (*queries, *fresh, *caches)
    nf = len(fresh)
    return pl.pallas_call(
        functools.partial(attend_kernel, rows, slots, nf),
        out_shape=[jax.ShapeDtypeStruct((rows + 32, 2 * HEAD), BF)] * Z,
        in_specs=[
            pl.BlockSpec(memory_space=pltpu.SMEM),
            pl.BlockSpec(memory_space=pltpu.VMEM),
            pl.BlockSpec(memory_space=pltpu.VMEM),
        ]
        + [any_spec] * len(operands),
        out_specs=[any_spec] * Z,
        scratch_shapes=[
            pltpu.VMEM((Z, 2 * rows, HEAD), BF),
            pltpu.VMEM((2, 2, rows, HEAD), BF),
            pltpu.VMEM((2, keys, HEAD), BF),
            pltpu.VMEM((2, keys, 2 * HEAD), BF),
            pltpu.VMEM((2, 2 * slots, HEAD), BF),
            pltpu.VMEM((2 * slots, HEAD), F32),
            pltpu.VMEM((Z, rows + 32, 2 * HEAD), BF),
            pltpu.VMEM((2, rows, HEAD), F32),
            pltpu.VMEM((2, rows, 2 * HEAD), F32),
            pltpu.SemaphoreType.DMA((Z,)),
            pltpu.SemaphoreType.DMA((max(2 * nf, 1),)),
            pltpu.SemaphoreType.DMA((max(2 * nf, 1),)),
            pltpu.SemaphoreType.DMA((2,)),
            pltpu.SemaphoreType.DMA((Z,)),
        ],
        compiler_params=pltpu.CompilerParams(vmem_limit_bytes=40 << 20),
        cost_estimate=pl.CostEstimate(
            flops=6_000_000_000, bytes_accessed=8_000_000, transcendentals=8_000_000
        ),
        name="attend",
    )(sc, turn, dec, *operands)


def shift(value, axis, size, step):
    return lax.ppermute(value, axis, [(i, (i + step) % size) for i in range(size)])


def layer_norm(inputs, ln_gain, ln_bias):
    values = inputs.astype(F32)
    center = jnp.mean(values, axis=-1, keepdims=True)
    spread = jnp.mean(jnp.square(values - center), axis=-1, keepdims=True)
    return ((values - center) * lax.rsqrt(spread + 1e-05) * ln_gain + ln_bias).astype(BF)


def rotary(vectors, cosine, sine):
    half = ROT // 2
    first, second, rest = vectors[..., :half], vectors[..., half:ROT], vectors[..., ROT:]
    return jnp.concatenate(
        [first * cosine - second * sine, second * cosine + first * sine, rest], axis=-1
    )


def decode_kernel(q_ref, cos_ref, sin_ref, info_ref, owner_ref, kv_ref, out_ref):
    owner = owner_ref[...]
    first, second, head = info_ref[:, 0:1], info_ref[:, 1:2], info_ref[:, 2:3]
    parity = lax.broadcasted_iota(I32, owner.shape, 1) & 1
    mask = ((owner == first) | (owner == second)) & (parity == head)
    q = turned(q_ref[...].astype(F32), cos_ref[...], sin_ref[...]).astype(BF)
    scores = jnp.where(mask, nt_dot(q, kv_ref[0]), NEG)
    top = jnp.maximum(jnp.max(scores, axis=1, keepdims=True), LOW)
    p = jnp.exp2((scores - top) * SCALE)
    out_ref[:, :HEAD] = jnp.dot(p.astype(BF), kv_ref[1], preferred_element_type=F32)
    lane = lax.broadcasted_iota(I32, (out_ref.shape[0], HEAD), 1)
    total = jnp.sum(p, axis=1, keepdims=True)
    out_ref[:, HEAD:] = jnp.where(lane == 0, top, jnp.where(lane == 1, total, 0.0))


def decode_attend(queries, cosine, sine, info, owner, kv):
    count = queries.shape[0]
    return pl.pallas_call(
        decode_kernel,
        out_shape=jax.ShapeDtypeStruct((count, 2 * HEAD), F32),
        cost_estimate=pl.CostEstimate(
            flops=110_000_000, bytes_accessed=1_000_000, transcendentals=210_000
        ),
        name="decode_attend",
    )(queries, cosine, sine, info, owner, kv)


def merge_parts(parts):
    parts = jnp.stack(parts)
    tops = parts[..., HEAD : HEAD + 1]
    top = jnp.max(tops, axis=0)
    scaled = parts * jnp.exp2((tops - top) * SCALE)
    total = jnp.sum(scaled, axis=0)
    lane = lax.broadcasted_iota(I32, total.shape, total.ndim - 1)
    return jnp.where(lane == HEAD, top, total)


def combine_kernel(rows, dec, self_ref, *refs):
    msgs, out_ref = refs[:-1], refs[-1]
    n = len(msgs)
    stats = [m[pl.ds(rows, 16), :].astype(F32) for m in msgs]
    weights = []
    for h in range(2):
        tops = [
            s[5 * h : 5 * h + 1] + s[5 * h + 1 : 5 * h + 2] + s[5 * h + 2 : 5 * h + 3]
            for s in stats
        ]
        totals = [s[5 * h + 3 : 5 * h + 4] + s[5 * h + 4 : 5 * h + 5] for s in stats]
        top = functools.reduce(jnp.maximum, tops)
        shares = [t * jnp.exp2((m - top) * SCALE) for m, t in zip(tops, totals)]
        inverse = 1.0 / functools.reduce(jnp.add, shares)
        weights += [s * inverse for s in shares]
    table = jnp.concatenate(weights + [jnp.zeros((HEAD - 2 * n, rows), F32)], axis=0)
    columns = jnp.transpose(table)
    for h in range(2):
        total = jnp.zeros((rows, HEAD), F32)
        for i, m in enumerate(msgs):
            k = h * n + i
            total += columns[:, k : k + 1] * m[pl.ds(0, rows), pl.ds(h * HEAD, HEAD)].astype(F32)
        out_ref[pl.ds(0, rows), h * HEAD : (h + 1) * HEAD] = total.astype(BF)

    values, tops, totals = [], [], []
    for m in msgs:
        part = m[pl.ds(rows + 16, 16), :].astype(F32)
        values.append(part[:, :HEAD])
        tops.append(
            part[:, HEAD : HEAD + 1] + part[:, HEAD + 1 : HEAD + 2] + part[:, HEAD + 2 : HEAD + 3]
        )
        totals.append(part[:, HEAD + 3 : HEAD + 4] + part[:, HEAD + 4 : HEAD + 5])
    mine = self_ref[...]
    values.append(mine[:, :HEAD])
    tops.append(mine[:, HEAD : HEAD + 1])
    totals.append(mine[:, HEAD + 1 : HEAD + 2])
    top = functools.reduce(jnp.maximum, tops)
    shares = [t * jnp.exp2((m - top) * SCALE) for m, t in zip(tops, totals)]
    whole = functools.reduce(jnp.add, shares)
    mixed = functools.reduce(jnp.add, [s * v for s, v in zip(shares, values)])
    mixed = mixed / jnp.where(whole > 0, whole, 1.0)
    out_ref[pl.ds(rows, 16), :HEAD] = mixed.astype(BF)
    out_ref[pl.ds(rows, 16), HEAD:] = pltpu.roll(mixed, 16 - dec, 0).astype(BF)


def combine(mine, msgs, dec):
    rows = msgs[0].shape[0] - 32
    return pl.pallas_call(
        functools.partial(combine_kernel, rows, dec),
        out_shape=jax.ShapeDtypeStruct((rows + 16, 2 * HEAD), BF),
        cost_estimate=pl.CostEstimate(
            flops=2_000_000, bytes_accessed=1_300_000, transcendentals=10_000
        ),
        name="combine",
    )(mine, *msgs)


def project_kernel(sc, parts, w_ref, bias_ref, out_ref, dec_ref):
    y = sc[0]
    total = jnp.zeros((parts.shape[2], out_ref.shape[1]), F32)
    for r in range(Y):
        yy = lax.rem(y - r + Y, Y)
        for c in range(C):
            total += jnp.dot(parts[c, r], w_ref[yy * C + c], preferred_element_type=F32)
    total = (total + bias_ref[...]).astype(BF)
    out_ref[...] = total[: out_ref.shape[0]]
    dec_ref[...] = total[out_ref.shape[0] :][: dec_ref.shape[0]]


def project(sc, parts, w, bias, rows, dec):
    vmem = pl.BlockSpec(memory_space=pltpu.VMEM)
    return pl.pallas_call(
        project_kernel,
        out_shape=[
            jax.ShapeDtypeStruct((rows, w.shape[2]), BF),
            jax.ShapeDtypeStruct((dec, w.shape[2]), BF),
        ],
        in_specs=[pl.BlockSpec(memory_space=pltpu.SMEM), vmem, vmem, vmem],
        out_specs=[vmem, vmem],
        cost_estimate=pl.CostEstimate(
            flops=550_000_000, bytes_accessed=3_500_000, transcendentals=0
        ),
        name="project",
    )(sc, parts, w, bias)


def merge_messages(a, b, rows):
    def parse(m):
        stats = m[:, rows : rows + 16].astype(F32)
        out = []
        for h in range(2):
            s = stats[:, 5 * h : 5 * h + 5]
            out.append((s[:, 0] + s[:, 1] + s[:, 2], s[:, 3] + s[:, 4]))
        return out

    results, stat_rows = [], []
    for h, ((ma, la), (mb, lb)) in enumerate(zip(parse(a), parse(b))):
        top = jnp.maximum(ma, mb)
        wa = la * jnp.exp2((ma - top) * SCALE)
        wb = lb * jnp.exp2((mb - top) * SCALE)
        total = wa + wb
        inverse = 1.0 / jnp.where(total > 0, total, 1.0)
        part = slice(h * HEAD, (h + 1) * HEAD)
        results.append(
            (wa * inverse)[..., None] * a[:, :rows, part].astype(F32)
            + (wb * inverse)[..., None] * b[:, :rows, part].astype(F32)
        )
        for value, count in ((top, 3), (total, 2)):
            for _ in range(count):
                piece = lax.reduce_precision(value, 8, 7)
                stat_rows.append(piece)
                value = value - piece
    stat_rows += [jnp.zeros_like(stat_rows[0])] * 6
    return jnp.concatenate(
        [
            jnp.concatenate(results, axis=2).astype(BF),
            jnp.stack(stat_rows, axis=1).astype(BF),
            a[:, rows + 16 :],
        ],
        axis=1,
    )


def on_device(
    prefill_x,
    decode_x,
    ln_gain,
    ln_bias,
    wqkv,
    qkv_bias,
    dense_w,
    dense_bias,
    kv_cache,
    slot_owner,
    group_of,
    span_lens,
):
    x, z = lax.axis_index("x"), lax.axis_index("z")
    y = lax.axis_index("y")
    rows, dec = prefill_x.shape[0], decode_x.shape[0]
    slots = slot_owner.shape[0]
    requests = group_of.shape[0]
    owners = SPANS + GROUPS + requests
    cache = kv_cache.reshape(2, 2 * slots, HEAD)

    cache_1 = lax.ppermute(cache, "x", [(0, 1)])
    cache_3 = lax.ppermute(cache, "x", [(0, 3)])

    owner_ids = jnp.arange(HEAD, dtype=I32)
    hits = (slot_owner[:, None] == owner_ids[None, :]) & (owner_ids < owners)[None, :]
    local = jnp.sum(hits.astype(F32), axis=0)
    begin = jnp.min(
        jnp.where(hits[:, :SPANS], jnp.arange(slots, dtype=I32)[:, None], slots), axis=0
    ).astype(F32)
    bounds = jnp.concatenate([begin, begin + local[:SPANS]])
    extra = jnp.where(x > 0, jnp.sum(local[:SPANS]), 0.0)
    vector = jnp.where(owner_ids == HEAD - 1, extra, local)
    at_row = jnp.where(x == 0, jnp.pad(bounds, (0, HEAD - 2 * SPANS)), 0.0)

    def split(values, unit):
        high = jnp.floor(values / unit)
        return [high, values - unit * high]

    count_rows = jnp.stack(split(vector, 16.0) + split(at_row, 16.0))
    count_rows = jnp.pad(count_rows, ((0, 12 - 2 * dec), (0, 0))).astype(BF)

    index = x * Z + z
    ends = jnp.cumsum(span_lens)
    begins = ends - span_lens
    token = index * rows + jnp.arange(rows, dtype=I32)
    offset = token - jnp.where(
        token >= ends[1], begins[2], jnp.where(token >= ends[0], begins[1], 0)
    )
    power = jnp.power(F32(10000.0), jnp.arange(ROT // 2, dtype=F32) * (-2.0 / ROT))
    angles = offset.astype(F32)[:, None] * power[None, :]
    cosine, sine = lax.optimization_barrier((jnp.cos(angles), jnp.sin(angles)))
    normed = layer_norm(jnp.concatenate([prefill_x, decode_x], axis=0), ln_gain, ln_bias)
    normed = lax.optimization_barrier(normed)
    pq = jnp.einsum("td,dhe->hte", normed, wqkv[:, :, 0], preferred_element_type=F32)
    pq = pq + qkv_bias[:, 0][:, None, :]
    my_q = rotary(pq[:, :rows], cosine, sine).astype(BF).reshape(2 * rows, HEAD)
    dec_q = pq[:, rows:].astype(BF).reshape(2 * dec, HEAD)

    first = jnp.concatenate([dec_q, count_rows], axis=0)
    normed, first = lax.optimization_barrier((normed, first))
    rounds = [first] + [shift(first, "x", X, r) for r in range(1, X)]
    pkv = jnp.einsum("td,dhje->jhte", normed, wqkv[:, :, 1:], preferred_element_type=F32)
    pkv = pkv + qkv_bias[:, 1:].transpose(1, 0, 2)[:, :, None, :]
    keys = rotary(pkv[0, :, :rows], cosine, sine).astype(BF)
    fresh = jnp.stack([keys, pkv[1, :, :rows].astype(BF)])
    at = 2 * dec
    numbers = [m[at : at + 4].astype(F32) for m in rounds]
    counted = functools.reduce(jnp.add, [16.0 * m[0] + m[1] for m in numbers])
    ranges = functools.reduce(jnp.add, [16.0 * m[2] + m[3] for m in numbers])

    second = jnp.concatenate(
        [my_q]
        + [m[:at] for m in rounds]
        + [jnp.pad(jnp.stack(split(counted, 32.0)), ((0, 14), (0, 0))).astype(BF)],
        axis=0,
    )
    all_q = [second] + [shift(second, "z", Z, s) for s in range(1, Z)]
    all_kv = [fresh] + [
        lax.ppermute(fresh, "x", [(i, i + r) for i in range(X - r)]) for r in (1, 2)
    ]
    half_1, half_3, _ = lax.optimization_barrier((cache_1[0], cache_3[1], fresh))
    cache_2k = lax.ppermute(half_1, "x", [(1, 2)])
    cache_2v = lax.ppermute(half_3, "x", [(3, 2)])

    width = dense_w.shape[2]
    held_w, _ = lax.optimization_barrier((dense_w, second))
    w_out = held_w.reshape(2 * HEAD, Y * C, width // (Y * C)).transpose(1, 0, 2)
    w_out = lax.all_to_all(w_out, ("y", "core"), 0, 0)

    dec_k = pkv[0, :, rows:].astype(BF).reshape(at, HEAD).astype(F32)
    dec_v = pkv[1, :, rows:].astype(BF).reshape(at, HEAD).astype(F32)
    self_score = jnp.sum(dec_q.astype(F32) * dec_k, axis=1, keepdims=True)
    mine = jnp.concatenate(
        [dec_v, self_score, jnp.ones_like(self_score), jnp.zeros((at, HEAD - 2), F32)], axis=1
    )
    mine = jnp.pad(mine, ((0, 16 - at), (0, 0)))

    row = jnp.arange(Z * X * at, dtype=I32)
    from_s, from_r = row // (X * at), (row // at) % X
    row_head, row_i = (row // dec) % 2, row % dec
    row_req = (((x - from_r + X) % X) * Z + (z - from_s + Z) % Z) * dec + row_i
    row_group = jnp.sum(
        jnp.where(row_req[:, None] == jnp.arange(requests, dtype=I32), group_of[None, :], 0), axis=1
    )
    labels = [SPANS + row_group, SPANS + GROUPS + row_req]
    info = jnp.stack(labels + [row_head], axis=1)
    span_row = jnp.arange(16, dtype=I32)
    picks = (
        (owner_ids[None, :] == jnp.concatenate([labels[0], span_row])[:, None])
        | (owner_ids[None, :] == jnp.concatenate([labels[1], span_row])[:, None])
    ).astype(F32)
    lane = jnp.arange(HEAD, dtype=I32)
    power_lanes = jnp.where(lane < ROT, jnp.tile(power, HEAD // (ROT // 2)), 0.0)
    signs = jnp.where(lane < ROT // 2, -1.0, 1.0).astype(F32)
    owner_row = jnp.repeat(slot_owner, 2)[None, :]
    picks, info, owner_row, mine = lax.optimization_barrier((picks, info, owner_row, mine))

    arrived = [m[2 * rows + 4 * at :].astype(F32) for m in all_q]
    counts = functools.reduce(jnp.add, [32.0 * m[0] + m[1] for m in arrived])
    more = counts[HEAD - 1] > 0
    position = jnp.sum(jnp.where(picks > 0, counts[None, :], 0.0), axis=1)
    turn_angle = position[:, None] * power_lanes[None, :]
    turn_cos, turn_sin = jnp.cos(turn_angle), jnp.sin(turn_angle) * signs
    n = Z * X * at
    everyone = jnp.concatenate([m[2 * rows : 2 * rows + 4 * at] for m in all_q], axis=0)
    parts = decode_attend(everyone, turn_cos[:n], turn_sin[:n], info, owner_row, cache)
    parts = parts.reshape(Z, X, at, 2 * HEAD)
    part_x = merge_parts(
        [parts[:, 0]] + [shift(parts[:, r], "x", X, X - r) for r in range(1, X)]
    )
    part_x = jnp.pad(part_x, ((0, 0), (0, 16 - at), (0, 0)))

    turn = jnp.concatenate([turn_cos[n : n + 4], turn_sin[n : n + 4]], axis=0)

    def scalars(limits):
        limits = jnp.stack([limits[:SPANS], limits[SPANS : 2 * SPANS]], axis=1).reshape(-1)
        return jnp.concatenate([jnp.stack([x, z]), ends[: SPANS - 1], limits.astype(I32)]).astype(
            I32
        )

    def general(msgs):
        def step(i, state):
            msgs, held, limits, row_of = state
            limits_now = jnp.where(row_of > 0, limits, jnp.zeros_like(limits))
            five = (held, held, held, held[0], held[1])
            found = attend(scalars(limits_now), turn, part_x, all_q, [], five)
            return (
                merge_messages(msgs, jnp.stack(found), rows),
                shift(held, "x", X, 1),
                shift(limits, "x", X, 1),
                shift(row_of, "x", X, 1),
            )

        state = (jnp.stack(msgs), cache, bounds.astype(I32), x)
        return tuple(lax.fori_loop(0, X, step, state)[0])

    caches = (cache, cache_1, cache_3, cache_2k, cache_2v)
    msgs = tuple(attend(scalars(ranges), turn, part_x, all_q, all_kv, caches))
    msgs = lax.while_loop(
        lambda state: state[0],
        lambda state: (jnp.zeros((), bool), general(state[1])),
        (more, msgs),
    )[1]
    home = [msgs[0]] + [shift(msgs[s], "z", Z, Z - s) for s in range(1, Z)]
    attended = combine(mine, home, dec)

    over_y = jnp.stack([attended] + [shift(attended, "y", Y, r) for r in range(1, Y)])
    gathered = lax.all_gather(over_y, "core")
    return tuple(
        project(y[None].astype(I32), gathered, w_out, dense_bias[None, :], rows, dec)
    )


def solution(mesh):
    mesh = Mesh(mesh.devices.reshape(X, Z, Y, C), ("x", "z", "y", "core"))
    seq, tensor = ("x", "z"), ("y", "core")
    in_specs = (
        P(seq, None),
        P(seq, None),
        P(),
        P(),
        P(None, tensor, None, None),
        P(tensor, None, None),
        P(tensor, None, None),
        P(tensor),
        P(None, seq, tensor, None),
        P(seq),
        P(),
        P(),
    )
    out_specs = (P(seq, tensor), P(seq, tensor))
    return jax.shard_map(
        on_device, mesh=mesh, in_specs=in_specs, out_specs=out_specs, check_vma=False
    )
```

```python
import functools
import math

import jax
import jax.numpy as jnp
from jax import lax
from jax.experimental import pallas as pl
from jax.experimental.pallas import tpu as pltpu
from jax.sharding import Mesh
from jax.sharding import PartitionSpec as P


X, Z, Y, C = 4, 8, 4, 2
SPANS, GROUPS, ROT = 3, 8, 32
HEAD = 128
NEG = -1e30
LOW = -1e29
SCALE = math.log2(math.e) / math.sqrt(HEAD)
BF, F32, I32 = jnp.bfloat16, jnp.float32, jnp.int32
TILE = 256

def pieces(value, count):
    out = []
    for _ in range(count):
        part = value.astype(BF).astype(F32)
        out.append(part)
        value = value - part
    return out


def nt_dot(a, b):
    return lax.dot_general(a, b, (((1,), (1,)), ((), ())), preferred_element_type=F32)


def turned(values, cosine, sine):
    lane = lax.broadcasted_iota(I32, values.shape, 1)
    half = ROT // 2
    partner = jnp.where(
        lane < half, pltpu.roll(values, HEAD - half, 1), pltpu.roll(values, half, 1)
    )
    return values * cosine + partner * sine


def attend_kernel(rows, slots, fresh, sc, turn_ref, *refs):
    nq = Z
    dec_refs, refs = refs[:X], refs[X:]
    q_refs, refs = refs[:nq], refs[nq:]
    kv_refs, refs = refs[:fresh], refs[fresh:]
    cache_refs, refs = refs[:5], refs[5:]
    out_refs, refs = refs[:nq], refs[nq:]
    qs, qx, kk, vv, cs, wide, msg, m_s, acc_s, q_sem, k_sem, v_sem, c_sem, o_sem = refs
    x, z = sc[0], sc[1]
    starts = (0, sc[2], sc[3])
    ends = (sc[2], sc[3], X * Z * rows)
    lows = (sc[4], sc[6], sc[8])
    highs = (sc[5], sc[7], sc[9])
    old = fresh * rows

    for t in range(2):
        for where_x, ref in ((0, cache_refs[0]), (1, cache_refs[1]), (3, cache_refs[2])):
            @pl.when(x == where_x)
            def _():
                pltpu.make_async_copy(ref.at[t], cs.at[t], c_sem.at[t]).start()

        @pl.when(x == 2)
        def _():
            pltpu.make_async_copy(cache_refs[3 + t], cs.at[t], c_sem.at[t]).start()

    for s in range(nq):
        pltpu.make_async_copy(q_refs[s].at[pl.ds(0, 2 * rows)], qs.at[s], q_sem.at[s]).start()
    k_copies, v_copies = [], []
    for r in range(fresh):
        for h in range(2):
            k_copies.append(
                pltpu.make_async_copy(
                    kv_refs[r].at[0, h], kk.at[h, pl.ds(r * rows, rows)], k_sem.at[2 * r + h]
                )
            )
            v_copies.append(
                pltpu.make_async_copy(
                    kv_refs[r].at[1, h],
                    vv.at[h, pl.ds(r * rows, rows), pl.ds(0, HEAD)],
                    v_sem.at[2 * r + h],
                )
            )
    for c in k_copies + v_copies:
        c.start()
    vv[:, :, HEAD:] = jnp.ones((2, vv.shape[1], HEAD), BF)
    spare = vv.shape[1] - old - slots
    if spare:
        kk[:, pl.ds(old + slots, spare), :] = jnp.zeros((2, spare, HEAD), BF)
        vv[:, pl.ds(old + slots, spare), :HEAD] = jnp.zeros((2, spare, HEAD), BF)

    pltpu.make_async_copy(cache_refs[3], cs.at[0], c_sem.at[0]).wait()
    wide[...] = cs[0].astype(F32)
    for h in range(2):
        kk[h, pl.ds(old, slots), :] = wide[pl.ds(h, slots, stride=2), :].astype(BF)
    pltpu.make_async_copy(cache_refs[4], cs.at[1], c_sem.at[1]).wait()
    wide[...] = cs[1].astype(F32)
    for h in range(2):
        vv[h, pl.ds(old, slots), :HEAD] = wide[pl.ds(h, slots, stride=2), :].astype(BF)
    for c in k_copies + v_copies:
        c.wait()

    def block(s, carry):
        pltpu.make_async_copy(q_refs[0].at[pl.ds(0, 2 * rows)], qs.at[s], q_sem.at[s]).wait()
        zq = lax.rem(z - s + Z, Z)
        base = (x * Z + zq) * rows
        qt = base + lax.broadcasted_iota(I32, (rows, 1), 0)
        second, third = qt >= starts[1], qt >= starts[2]

        def pick(a):
            return jnp.where(third, a[2], jnp.where(second, a[1], a[0]))

        start_q, lo_q, hi_q = pick(starts), pick(lows), pick(highs)
        first_start = jnp.where(
            base >= starts[2], starts[2], jnp.where(base >= starts[1], starts[1], 0)
        )
        last_start = jnp.where(
            base + rows > starts[2],
            starts[2],
            jnp.where(base + rows > starts[1], starts[1], 0),
        )
        cosine = pick([turn_ref[pl.ds(c, 1), :] for c in range(SPANS)])
        sine = pick([turn_ref[pl.ds(4 + c, 1), :] for c in range(SPANS)])
        for h in range(2):
            q = qs[s, pl.ds(h * rows, rows), :]
            qx[0, h] = q
            qx[1, h] = turned(q.astype(F32), cosine, sine).astype(BF)
        m_s[...] = jnp.full_like(m_s, LOW)
        acc_s[...] = jnp.zeros_like(acc_s)
        any_lo, any_hi, all_lo, all_hi = slots, 0, 0, slots
        for c in range(SPANS):
            here = (base < ends[c]) & (base + rows > starts[c])
            some = here & (highs[c] > lows[c])
            any_lo = jnp.where(some, jnp.minimum(any_lo, lows[c]), any_lo)
            any_hi = jnp.where(some, jnp.maximum(any_hi, highs[c]), any_hi)
            all_lo = jnp.where(here, jnp.maximum(all_lo, lows[c]), all_lo)
            all_hi = jnp.where(here, jnp.minimum(all_hi, highs[c]), all_hi)

        def tile(j, carry):
            is_old = j >= fresh
            kb = jnp.where(is_old, (j - fresh) * TILE, ((x - j) * Z + z) * rows)
            need_new = (x >= j) & (kb <= base + rows - 1) & (kb + TILE > first_start)
            full_new = (kb + TILE - 1 <= base) & (kb >= last_start)
            need_old = (kb < any_hi) & (kb + TILE > any_lo)
            full_old = (kb >= all_lo) & (kb + TILE <= all_hi)
            need = jnp.where(is_old, need_old, need_new)
            full = jnp.where(is_old, full_old, full_new)
            which = jnp.where(is_old, 1, 0)
            at = pl.multiple_of(j * TILE, TILE)

            def update(mask):
                all_s = [nt_dot(qx[which, h], kk[h, pl.ds(at, TILE), :]) for h in range(2)]
                if mask is not None:
                    all_s = [jnp.where(mask, s_, NEG) for s_ in all_s]
                tops = [jnp.max(s_, axis=1, keepdims=True) for s_ in all_s]
                ps = []
                for h in range(2):
                    m_old = m_s[h]
                    m_new = jnp.maximum(m_old, tops[h])
                    alpha = jnp.exp2((m_old - m_new) * SCALE)
                    wide_m = jnp.concatenate([m_new] * (TILE // HEAD), axis=1)
                    ps.append((jnp.exp2((all_s[h] - wide_m) * SCALE).astype(BF), alpha))
                    m_s[h] = m_new
                for h in range(2):
                    p, alpha = ps[h]
                    acc_s[h] = jnp.concatenate([alpha, alpha], axis=1) * acc_s[h] + jnp.dot(
                        p, vv[h, pl.ds(at, TILE), :], preferred_element_type=F32
                    )

            @pl.when(need & full)
            def _():
                update(None)

            @pl.when(need & jnp.logical_not(full))
            def _():
                key = kb + lax.broadcasted_iota(I32, (1, TILE), 1)
                low = jnp.where(is_old, lo_q, start_q)
                high = jnp.where(is_old, hi_q - 1, qt)
                update((key >= low) & (key <= high))

            return carry

        lax.fori_loop(0, kk.shape[1] // TILE, tile, 0)

        lane = lax.broadcasted_iota(I32, (rows, HEAD), 1)
        stats = jnp.zeros((rows, HEAD), F32)
        for h in range(2):
            total = acc_s[h, :, HEAD:]
            inverse = 1.0 / jnp.where(total > 0, total, 1.0)
            msg[s, pl.ds(0, rows), pl.ds(h * HEAD, HEAD)] = (acc_s[h, :, :HEAD] * inverse).astype(BF)
            for k, part in enumerate(pieces(m_s[h], 3) + pieces(total, 2)):
                stats = jnp.where(lane == 5 * h + k, part, stats)
        msg[s, pl.ds(rows, 16), :] = jnp.transpose(stats)[:16].astype(BF)
        found = [d[pl.ds(pl.multiple_of(s * 8, 8), 8), :] for d in dec_refs]
        top = functools.reduce(jnp.maximum, [f[:, HEAD : HEAD + 1] for f in found])
        found = [f * jnp.exp2((f[:, HEAD : HEAD + 1] - top) * SCALE) for f in found]
        part = functools.reduce(jnp.add, found)
        total = part[:, HEAD + 1 : HEAD + 2]
        inverse = 1.0 / jnp.where(total > 0, total, 1.0)
        lane = lax.broadcasted_iota(I32, (8, HEAD), 1)
        stats = jnp.zeros((8, HEAD), F32)
        for k, piece in enumerate(pieces(top, 3) + pieces(total, 2)):
            stats = jnp.where(lane == k, piece, stats)
        part = jnp.concatenate([part[:, :HEAD] * inverse, stats], axis=1)
        msg[s, pl.ds(rows + 16, 16), :] = jnp.concatenate(
            [part, jnp.zeros_like(part)], axis=0
        ).astype(BF)
        for k in range(nq):
            @pl.when(s == k)
            def _():
                pltpu.make_async_copy(msg.at[k], out_refs[k], o_sem.at[k]).start()
        return carry

    lax.fori_loop(0, nq, block, 0)
    for s in range(nq):
        pltpu.make_async_copy(msg.at[s], out_refs[s], o_sem.at[s]).wait()


def attend(sc, turn, dec, queries, fresh, caches):
    rows = fresh[0].shape[2] if fresh else TILE
    slots = caches[0].shape[1] // 2
    keys = len(fresh) * rows + -(-slots // TILE) * TILE
    any_spec = pl.BlockSpec(memory_space=pl.ANY)
    operands = (*queries, *fresh, *caches)
    nf = len(fresh)
    return pl.pallas_call(
        functools.partial(attend_kernel, rows, slots, nf),
        out_shape=[jax.ShapeDtypeStruct((rows + 32, 2 * HEAD), BF)] * Z,
        in_specs=[
            pl.BlockSpec(memory_space=pltpu.SMEM),
        ]
        + [pl.BlockSpec(memory_space=pltpu.VMEM)] * (1 + X)
        + [any_spec] * len(operands),
        out_specs=[any_spec] * Z,
        scratch_shapes=[
            pltpu.VMEM((Z, 2 * rows, HEAD), BF),
            pltpu.VMEM((2, 2, rows, HEAD), BF),
            pltpu.VMEM((2, keys, HEAD), BF),
            pltpu.VMEM((2, keys, 2 * HEAD), BF),
            pltpu.VMEM((2, 2 * slots, HEAD), BF),
            pltpu.VMEM((2 * slots, HEAD), F32),
            pltpu.VMEM((Z, rows + 32, 2 * HEAD), BF),
            pltpu.VMEM((2, rows, HEAD), F32),
            pltpu.VMEM((2, rows, 2 * HEAD), F32),
            pltpu.SemaphoreType.DMA((Z,)),
            pltpu.SemaphoreType.DMA((max(2 * nf, 1),)),
            pltpu.SemaphoreType.DMA((max(2 * nf, 1),)),
            pltpu.SemaphoreType.DMA((2,)),
            pltpu.SemaphoreType.DMA((Z,)),
        ],
        compiler_params=pltpu.CompilerParams(vmem_limit_bytes=40 << 20),
        cost_estimate=pl.CostEstimate(
            flops=6_000_000_000, bytes_accessed=8_000_000, transcendentals=8_000_000
        ),
        name="attend",
    )(sc, turn, *dec, *operands)


def shift(value, axis, size, step):
    return lax.ppermute(value, axis, [(i, (i + step) % size) for i in range(size)])


def layer_norm(inputs, ln_gain, ln_bias):
    values = inputs.astype(F32)
    center = jnp.mean(values, axis=-1, keepdims=True)
    spread = jnp.mean(jnp.square(values - center), axis=-1, keepdims=True)
    return ((values - center) * lax.rsqrt(spread + 1e-05) * ln_gain + ln_bias).astype(BF)


def rotary(vectors, cosine, sine):
    half = ROT // 2
    first, second, rest = vectors[..., :half], vectors[..., half:ROT], vectors[..., ROT:]
    return jnp.concatenate(
        [first * cosine - second * sine, second * cosine + first * sine, rest], axis=-1
    )


def decode_kernel(start, picks_ref, info_ref, power_ref, owner_ref, kv_ref, *refs):
    msgs, refs = refs[:Z], refs[Z:]
    outs, refs = refs[:X], refs[X:]
    turn_ref, count_ref, rows_s, sem = refs
    copies = [
        pltpu.make_async_copy(m.at[pl.ds(start, 8 * X)], rows_s.at[s], sem.at[s])
        for s, m in enumerate(msgs)
    ]
    for c in copies:
        c.start()
    for c in copies:
        c.wait()
    n = Z * X * 8
    rows = rows_s[...].astype(F32).reshape(n, HEAD)
    counts = jnp.zeros((1, HEAD), F32)
    for s in range(Z):
        at = s * X * 8 + 4
        counts += 32.0 * rows[at : at + 1] + rows[at + 1 : at + 2]
    count_ref[...] = jnp.broadcast_to(counts, count_ref.shape)
    position = jnp.sum(jnp.where(picks_ref[...] > 0, counts, 0.0), axis=1, keepdims=True)
    angle = position * power_ref[0:1, :]
    cosine, sine = jnp.cos(angle), jnp.sin(angle) * power_ref[1:2, :]
    turn_ref[0:4, :] = cosine[n : n + 4]
    turn_ref[4:8, :] = sine[n : n + 4]
    q = turned(rows, cosine[:n], sine[:n]).astype(BF)
    owner = owner_ref[...]
    first, second, head = info_ref[:, 0:1], info_ref[:, 1:2], info_ref[:, 2:3]
    parity = lax.broadcasted_iota(I32, owner.shape, 1) & 1
    mask = ((owner == first) | (owner == second)) & (parity == head)
    scores = jnp.where(mask, nt_dot(q, kv_ref[0]), NEG)
    top = jnp.maximum(jnp.max(scores, axis=1, keepdims=True), LOW)
    p = jnp.exp2((scores - top) * SCALE)
    lane = lax.broadcasted_iota(I32, (n, HEAD), 1)
    total = jnp.sum(p, axis=1, keepdims=True)
    stats = jnp.where(lane == 0, top, jnp.where(lane == 1, total, 0.0))
    mixed = jnp.dot(p.astype(BF), kv_ref[1], preferred_element_type=F32)
    for s in range(Z):
        for r in range(X):
            at = (s * X + r) * 8
            outs[r][s * 8 : s * 8 + 8, :HEAD] = mixed[at : at + 8]
            outs[r][s * 8 : s * 8 + 8, HEAD:] = stats[at : at + 8]


def decode_attend(start, picks, info, power, owner, kv, msgs):
    vmem = pl.BlockSpec(memory_space=pltpu.VMEM)
    out = pl.pallas_call(
        functools.partial(decode_kernel, start),
        out_shape=[jax.ShapeDtypeStruct((Z * 8, 2 * HEAD), F32)] * X
        + [jax.ShapeDtypeStruct((8, HEAD), F32)] * 2,
        in_specs=[vmem] * 5 + [pl.BlockSpec(memory_space=pl.ANY)] * Z,
        out_specs=[vmem] * (X + 2),
        scratch_shapes=[
            pltpu.VMEM((Z, 8 * X, HEAD), BF),
            pltpu.SemaphoreType.DMA((Z,)),
        ],
        cost_estimate=pl.CostEstimate(
            flops=220_000_000, bytes_accessed=1_500_000, transcendentals=500_000
        ),
        name="decode_attend",
    )(picks, info, power, owner, kv, *msgs)
    return out[:X], out[X], out[X + 1]


def combine_kernel(rows, dec, self_ref, *refs):
    msgs, out_ref = refs[:-1], refs[-1]
    n = len(msgs)
    stats = [m[pl.ds(rows, 16), :].astype(F32) for m in msgs]
    weights = []
    for h in range(2):
        tops = [
            s[5 * h : 5 * h + 1] + s[5 * h + 1 : 5 * h + 2] + s[5 * h + 2 : 5 * h + 3]
            for s in stats
        ]
        totals = [s[5 * h + 3 : 5 * h + 4] + s[5 * h + 4 : 5 * h + 5] for s in stats]
        top = functools.reduce(jnp.maximum, tops)
        shares = [t * jnp.exp2((m - top) * SCALE) for m, t in zip(tops, totals)]
        inverse = 1.0 / functools.reduce(jnp.add, shares)
        weights += [s * inverse for s in shares]
    table = jnp.concatenate(weights + [jnp.zeros((HEAD - 2 * n, rows), F32)], axis=0)
    columns = jnp.transpose(table)
    for h in range(2):
        total = jnp.zeros((rows, HEAD), F32)
        for i, m in enumerate(msgs):
            k = h * n + i
            total += columns[:, k : k + 1] * m[pl.ds(0, rows), pl.ds(h * HEAD, HEAD)].astype(F32)
        out_ref[pl.ds(0, rows), h * HEAD : (h + 1) * HEAD] = total.astype(BF)

    values, tops, totals = [], [], []
    for m in msgs:
        part = m[pl.ds(rows + 16, 16), :].astype(F32)
        values.append(part[:, :HEAD])
        tops.append(
            part[:, HEAD : HEAD + 1] + part[:, HEAD + 1 : HEAD + 2] + part[:, HEAD + 2 : HEAD + 3]
        )
        totals.append(part[:, HEAD + 3 : HEAD + 4] + part[:, HEAD + 4 : HEAD + 5])
    mine = self_ref[...]
    values.append(mine[:, :HEAD])
    tops.append(mine[:, HEAD : HEAD + 1])
    totals.append(mine[:, HEAD + 1 : HEAD + 2])
    top = functools.reduce(jnp.maximum, tops)
    shares = [t * jnp.exp2((m - top) * SCALE) for m, t in zip(tops, totals)]
    whole = functools.reduce(jnp.add, shares)
    mixed = functools.reduce(jnp.add, [s * v for s, v in zip(shares, values)])
    mixed = mixed / jnp.where(whole > 0, whole, 1.0)
    out_ref[pl.ds(rows, 16), :HEAD] = mixed.astype(BF)
    out_ref[pl.ds(rows, 16), HEAD:] = pltpu.roll(mixed, 16 - dec, 0).astype(BF)


def combine(mine, msgs, dec):
    rows = msgs[0].shape[0] - 32
    return pl.pallas_call(
        functools.partial(combine_kernel, rows, dec),
        out_shape=jax.ShapeDtypeStruct((rows + 16, 2 * HEAD), BF),
        cost_estimate=pl.CostEstimate(
            flops=2_000_000, bytes_accessed=1_300_000, transcendentals=10_000
        ),
        name="combine",
    )(mine, *msgs)


def project_kernel(sc, *refs):
    parts, refs = refs[: 2 * Y], refs[2 * Y :]
    w_ref, bias_ref, out_ref, dec_ref = refs
    y, core = sc[0], sc[1]
    total = jnp.zeros((parts[0].shape[0], out_ref.shape[1]), F32)
    for k, part in enumerate(parts):
        r, c = k % Y, k // Y
        owner = lax.rem(y - r + Y, Y) * C + lax.rem(core + c, C)
        total += jnp.dot(part[...], w_ref[owner], preferred_element_type=F32)
    total = (total + bias_ref[...]).astype(BF)
    out_ref[...] = total[: out_ref.shape[0]]
    dec_ref[...] = total[out_ref.shape[0] :][: dec_ref.shape[0]]


def project(sc, parts, w, bias, rows, dec):
    vmem = pl.BlockSpec(memory_space=pltpu.VMEM)
    return pl.pallas_call(
        project_kernel,
        out_shape=[
            jax.ShapeDtypeStruct((rows, w.shape[2]), BF),
            jax.ShapeDtypeStruct((dec, w.shape[2]), BF),
        ],
        in_specs=[pl.BlockSpec(memory_space=pltpu.SMEM)] + [vmem] * (2 * Y + 2),
        out_specs=[vmem, vmem],
        cost_estimate=pl.CostEstimate(
            flops=550_000_000, bytes_accessed=3_500_000, transcendentals=0
        ),
        name="project",
    )(sc, *parts, w, bias)


def merge_messages(a, b, rows):
    def parse(m):
        stats = m[:, rows : rows + 16].astype(F32)
        out = []
        for h in range(2):
            s = stats[:, 5 * h : 5 * h + 5]
            out.append((s[:, 0] + s[:, 1] + s[:, 2], s[:, 3] + s[:, 4]))
        return out

    results, stat_rows = [], []
    for h, ((ma, la), (mb, lb)) in enumerate(zip(parse(a), parse(b))):
        top = jnp.maximum(ma, mb)
        wa = la * jnp.exp2((ma - top) * SCALE)
        wb = lb * jnp.exp2((mb - top) * SCALE)
        total = wa + wb
        inverse = 1.0 / jnp.where(total > 0, total, 1.0)
        part = slice(h * HEAD, (h + 1) * HEAD)
        results.append(
            (wa * inverse)[..., None] * a[:, :rows, part].astype(F32)
            + (wb * inverse)[..., None] * b[:, :rows, part].astype(F32)
        )
        for value, count in ((top, 3), (total, 2)):
            for _ in range(count):
                piece = lax.reduce_precision(value, 8, 7)
                stat_rows.append(piece)
                value = value - piece
    stat_rows += [jnp.zeros_like(stat_rows[0])] * 6
    return jnp.concatenate(
        [
            jnp.concatenate(results, axis=2).astype(BF),
            jnp.stack(stat_rows, axis=1).astype(BF),
            a[:, rows + 16 :],
        ],
        axis=1,
    )


def on_device(
    prefill_x,
    decode_x,
    ln_gain,
    ln_bias,
    wqkv,
    qkv_bias,
    dense_w,
    dense_bias,
    kv_cache,
    slot_owner,
    group_of,
    span_lens,
):
    x, z = lax.axis_index("x"), lax.axis_index("z")
    y, core = lax.axis_index("y"), lax.axis_index("core")
    rows, dec = prefill_x.shape[0], decode_x.shape[0]
    slots = slot_owner.shape[0]
    requests = group_of.shape[0]
    owners = SPANS + GROUPS + requests
    cache = kv_cache.reshape(2, 2 * slots, HEAD)

    cache_1 = lax.ppermute(cache, "x", [(0, 1)])
    cache_3 = lax.ppermute(cache, "x", [(0, 3)])

    owner_ids = jnp.arange(HEAD, dtype=I32)
    hits = (slot_owner[:, None] == owner_ids[None, :]) & (owner_ids < owners)[None, :]
    local = jnp.sum(hits.astype(F32), axis=0)
    begin = jnp.min(
        jnp.where(hits[:, :SPANS], jnp.arange(slots, dtype=I32)[:, None], slots), axis=0
    ).astype(F32)
    bounds = jnp.concatenate([begin, begin + local[:SPANS]])
    extra = jnp.where(x > 0, jnp.sum(local[:SPANS]), 0.0)
    vector = jnp.where(owner_ids == HEAD - 1, extra, local)
    at_row = jnp.where(x == 0, jnp.pad(bounds, (0, HEAD - 2 * SPANS)), 0.0)

    def split(values, unit):
        high = jnp.floor(values / unit)
        return [high, values - unit * high]

    count_rows = jnp.stack(split(vector, 16.0) + split(at_row, 16.0))
    count_rows = count_rows.astype(BF)

    index = x * Z + z
    ends = jnp.cumsum(span_lens)
    begins = ends - span_lens
    token = index * rows + jnp.arange(rows, dtype=I32)
    offset = token - jnp.where(
        token >= ends[1], begins[2], jnp.where(token >= ends[0], begins[1], 0)
    )
    power = jnp.power(F32(10000.0), jnp.arange(ROT // 2, dtype=F32) * (-2.0 / ROT))
    angles = offset.astype(F32)[:, None] * power[None, :]
    cosine, sine = lax.optimization_barrier((jnp.cos(angles), jnp.sin(angles)))
    normed = layer_norm(jnp.concatenate([prefill_x, decode_x], axis=0), ln_gain, ln_bias)
    normed = lax.optimization_barrier(normed)
    pq = jnp.einsum("td,dhe->hte", normed, wqkv[:, :, 0], preferred_element_type=F32)
    pq = pq + qkv_bias[:, 0][:, None, :]
    my_q = rotary(pq[:, :rows], cosine, sine).astype(BF).reshape(2 * rows, HEAD)
    dec_q = pq[:, rows:].astype(BF).reshape(2 * dec, HEAD)

    first = jnp.concatenate([dec_q, count_rows], axis=0)
    normed, first = lax.optimization_barrier((normed, first))
    rounds = [first] + [shift(first, "x", X, r) for r in range(1, X)]
    pkv = jnp.einsum("td,dhje->jhte", normed, wqkv[:, :, 1:], preferred_element_type=F32)
    pkv = pkv + qkv_bias[:, 1:].transpose(1, 0, 2)[:, :, None, :]
    keys = rotary(pkv[0, :, :rows], cosine, sine).astype(BF)
    fresh = jnp.stack([keys, pkv[1, :, :rows].astype(BF)])
    at = 2 * dec
    numbers = [m[at : at + 4].astype(F32) for m in rounds]
    counted = functools.reduce(jnp.add, [16.0 * m[0] + m[1] for m in numbers])
    ranges = functools.reduce(jnp.add, [16.0 * m[2] + m[3] for m in numbers])

    tails = [jnp.stack(split(counted, 32.0)).astype(BF)] + [jnp.zeros((2, HEAD), BF)] * (X - 1)
    gap = jnp.zeros((8 - at - 2, HEAD), BF)
    second = [my_q]
    for m, tail in zip(rounds, tails):
        second += [m[:at], tail, gap]
    second = jnp.concatenate(second, axis=0)
    second, fresh = lax.optimization_barrier((second, fresh))
    all_q = [second] + [shift(second, "z", Z, s) for s in range(1, Z)]
    all_kv = [fresh] + [
        lax.ppermute(fresh, "x", [(i, i + r) for i in range(X - r)]) for r in (1, 2)
    ]
    half_1, half_3, _ = lax.optimization_barrier((cache_1[0], cache_3[1], fresh))
    cache_2k = lax.ppermute(half_1, "x", [(1, 2)])
    cache_2v = lax.ppermute(half_3, "x", [(3, 2)])

    width = dense_w.shape[2]
    held_w, _ = lax.optimization_barrier((dense_w, second))
    w_out = held_w.reshape(2 * HEAD, Y * C, width // (Y * C)).transpose(1, 0, 2)
    w_out = lax.all_to_all(w_out, ("y", "core"), 0, 0)

    dec_k = pkv[0, :, rows:].astype(BF).reshape(at, HEAD).astype(F32)
    dec_v = pkv[1, :, rows:].astype(BF).reshape(at, HEAD).astype(F32)
    self_score = jnp.sum(dec_q.astype(F32) * dec_k, axis=1, keepdims=True)
    mine = jnp.concatenate(
        [dec_v, self_score, jnp.ones_like(self_score), jnp.zeros((at, HEAD - 2), F32)], axis=1
    )
    mine = jnp.pad(mine, ((0, 16 - at), (0, 0)))

    row = jnp.arange(Z * X * 8, dtype=I32)
    from_s, from_r, inner = row // (X * 8), (row // 8) % X, row % 8
    row_head, row_i = inner // dec, inner % dec
    row_req = (((x - from_r + X) % X) * Z + (z - from_s + Z) % Z) * dec + row_i
    row_group = jnp.sum(
        jnp.where(row_req[:, None] == jnp.arange(requests, dtype=I32), group_of[None, :], 0), axis=1
    )
    real = inner < at
    labels = [
        jnp.where(real, SPANS + row_group, -7),
        jnp.where(real, SPANS + GROUPS + row_req, -7),
    ]
    info = jnp.stack(labels + [row_head], axis=1)
    span_row = jnp.arange(16, dtype=I32)
    picks = (
        (owner_ids[None, :] == jnp.concatenate([labels[0], span_row])[:, None])
        | (owner_ids[None, :] == jnp.concatenate([labels[1], span_row])[:, None])
    ).astype(F32)
    lane = jnp.arange(HEAD, dtype=I32)
    power_lanes = jnp.where(lane < ROT, jnp.tile(power, HEAD // (ROT // 2)), 0.0)
    signs = jnp.where(lane < ROT // 2, -1.0, 1.0).astype(F32)
    power_rows = jnp.stack([power_lanes, signs])
    owner_row = jnp.repeat(slot_owner, 2)[None, :]
    picks, info, owner_row, mine, power_rows, _ = lax.optimization_barrier(
        (picks, info, owner_row, mine, power_rows, second)
    )

    ready = lax.optimization_barrier((tuple(all_q), cache_2k, cache_2v))
    all_q, cache_2k, cache_2v = ready
    parts, turn, counts = decode_attend(
        2 * rows, picks, info, power_rows, owner_row, cache, all_q
    )
    more = counts[0, HEAD - 1] > 0
    parts = [parts[0]] + [shift(parts[r], "x", X, X - r) for r in range(1, X)]

    def scalars(limits):
        limits = jnp.stack([limits[:SPANS], limits[SPANS : 2 * SPANS]], axis=1).reshape(-1)
        return jnp.concatenate([jnp.stack([x, z]), ends[: SPANS - 1], limits.astype(I32)]).astype(
            I32
        )

    def general(msgs):
        def step(i, state):
            msgs, held, limits, row_of = state
            limits_now = jnp.where(row_of > 0, limits, jnp.zeros_like(limits))
            five = (held, held, held, held[0], held[1])
            found = attend(scalars(limits_now), turn, parts, all_q, [], five)
            return (
                merge_messages(msgs, jnp.stack(found), rows),
                shift(held, "x", X, 1),
                shift(limits, "x", X, 1),
                shift(row_of, "x", X, 1),
            )

        state = (jnp.stack(msgs), cache, bounds.astype(I32), x)
        return tuple(lax.fori_loop(0, X, step, state)[0])

    caches = (cache, cache_1, cache_3, cache_2k, cache_2v)
    msgs = tuple(attend(scalars(ranges), turn, parts, all_q, all_kv, caches))
    msgs = lax.while_loop(
        lambda state: state[0],
        lambda state: (jnp.zeros((), bool), general(state[1])),
        (more, msgs),
    )[1]
    home = [msgs[0]] + [shift(msgs[s], "z", Z, Z - s) for s in range(1, Z)]
    attended = combine(mine, home, dec)

    over_y = [attended] + [shift(attended, "y", Y, r) for r in range(1, Y)]
    over_y += [lax.ppermute(v, "core", [(0, 1), (1, 0)]) for v in over_y]
    place = jnp.stack([y, core]).astype(I32)
    return tuple(project(place, over_y, w_out, dense_bias[None, :], rows, dec))


def solution(mesh):
    mesh = Mesh(mesh.devices.reshape(X, Z, Y, C), ("x", "z", "y", "core"))
    seq, tensor = ("x", "z"), ("y", "core")
    in_specs = (
        P(seq, None),
        P(seq, None),
        P(),
        P(),
        P(None, tensor, None, None),
        P(tensor, None, None),
        P(tensor, None, None),
        P(tensor),
        P(None, seq, tensor, None),
        P(seq),
        P(),
        P(),
    )
    out_specs = (P(seq, tensor), P(seq, tensor))
    return jax.shard_map(
        on_device, mesh=mesh, in_specs=in_specs, out_specs=out_specs, check_vma=False
    )
```

```python
import functools
import math

import jax
import jax.numpy as jnp
from jax import lax
from jax.experimental import pallas as pl
from jax.experimental.pallas import tpu as pltpu
from jax.sharding import Mesh
from jax.sharding import PartitionSpec as P


X, Z, Y, C = 4, 8, 4, 2
SPANS, GROUPS, ROT = 3, 8, 32
HEAD = 128
NEG = -1e30
LOW = -1e29
SCALE = math.log2(math.e) / math.sqrt(HEAD)
BF, F32, I32 = jnp.bfloat16, jnp.float32, jnp.int32
TILE = 256
OLD = 512


def pieces(value, count):
    out = []
    for _ in range(count):
        part = value.astype(BF).astype(F32)
        out.append(part)
        value = value - part
    return out


def nt_dot(a, b):
    return lax.dot_general(a, b, (((1,), (1,)), ((), ())), preferred_element_type=F32)


def turned(values, cosine, sine):
    lane = lax.broadcasted_iota(I32, values.shape, 1)
    half = ROT // 2
    partner = jnp.where(
        lane < half, pltpu.roll(values, HEAD - half, 1), pltpu.roll(values, half, 1)
    )
    return values * cosine + partner * sine


def attend_kernel(rows, slots, fresh, lens, sc, turn_ref, *refs):
    nq = Z
    dec_refs, refs = refs[:X], refs[X:]
    q_refs, refs = refs[:nq], refs[nq:]
    kv_refs, refs = refs[:fresh], refs[fresh:]
    cache_refs, refs = refs[:5], refs[5:]
    out_refs, refs = refs[:nq], refs[nq:]
    qs, qx, kk, vv, cs, wide, msg, m_s, acc_s, q_sem, k_sem, v_sem, c_sem, o_sem = refs
    x, z = lax.axis_index("x"), lax.axis_index("z")
    starts = (0, lens[0], lens[0] + lens[1])
    ends = (starts[1], starts[2], X * Z * rows)
    lows = (sc[0, 0], sc[0, 1], sc[0, 2])
    highs = (sc[0, 3], sc[0, 4], sc[0, 5])
    old = fresh * rows

    for t in range(2):
        for where_x, ref in ((0, cache_refs[0]), (1, cache_refs[1]), (3, cache_refs[2])):
            @pl.when(x == where_x)
            def _():
                pltpu.make_async_copy(ref.at[t], cs.at[t], c_sem.at[t]).start()

        @pl.when(x == 2)
        def _():
            pltpu.make_async_copy(cache_refs[3 + t], cs.at[t], c_sem.at[t]).start()

    for s in range(nq):
        pltpu.make_async_copy(q_refs[s].at[pl.ds(0, 2 * rows)], qs.at[s], q_sem.at[s]).start()
    k_copies, v_copies = [], []
    for r in range(fresh):
        for h in range(2):
            k_copies.append(
                pltpu.make_async_copy(
                    kv_refs[r].at[0, h], kk.at[h, pl.ds(r * rows, rows)], k_sem.at[2 * r + h]
                )
            )
            v_copies.append(
                pltpu.make_async_copy(
                    kv_refs[r].at[1, h],
                    vv.at[h, pl.ds(r * rows, rows), pl.ds(0, HEAD)],
                    v_sem.at[2 * r + h],
                )
            )
    for c in k_copies + v_copies:
        c.start()

    def fill(j, carry):
        part = pl.ds(pl.multiple_of(j * TILE, TILE), TILE)
        for h in range(2):
            vv[h, part, HEAD:] = jnp.ones((TILE, HEAD), BF)
        return carry

    lax.fori_loop(0, vv.shape[1] // TILE, fill, 0)
    spare = vv.shape[1] - old - slots
    if spare:
        kk[:, pl.ds(old + slots, spare), :] = jnp.zeros((2, spare, HEAD), BF)
        vv[:, pl.ds(old + slots, spare), :HEAD] = jnp.zeros((2, spare, HEAD), BF)

    piece_slots = wide.shape[0] // 2
    for t in range(2):
        pltpu.make_async_copy(cache_refs[3 + t], cs.at[t], c_sem.at[t]).wait()

        def part(c, carry):
            source = pl.multiple_of(c * 2 * piece_slots, 2 * piece_slots)
            target = pl.ds(pl.multiple_of(old + c * piece_slots, 16), piece_slots)
            wide[...] = cs[t, pl.ds(source, 2 * piece_slots), :].astype(F32)
            for h in range(2):
                values = wide[pl.ds(h, piece_slots, stride=2), :].astype(BF)
                if t == 0:
                    kk[h, target, :] = values
                else:
                    vv[h, target, :HEAD] = values
            return carry

        lax.fori_loop(0, slots // piece_slots, part, 0)
    for c in k_copies + v_copies:
        c.wait()

    def block(s, carry):
        pltpu.make_async_copy(q_refs[0].at[pl.ds(0, 2 * rows)], qs.at[s], q_sem.at[s]).wait()
        zq = lax.rem(z - s + Z, Z)
        base = (x * Z + zq) * rows
        qt = base + lax.broadcasted_iota(I32, (rows, 1), 0)
        second, third = qt >= starts[1], qt >= starts[2]

        def pick(a):
            return jnp.where(third, a[2], jnp.where(second, a[1], a[0]))

        start_q, lo_q, hi_q = pick(starts), pick(lows), pick(highs)
        first_start = jnp.where(
            base >= starts[2], starts[2], jnp.where(base >= starts[1], starts[1], 0)
        )
        cosine = pick([turn_ref[pl.ds(c, 1), :] for c in range(SPANS)])
        sine = pick([turn_ref[pl.ds(4 + c, 1), :] for c in range(SPANS)])
        for h in range(2):
            q = qs[s, pl.ds(h * rows, rows), :]
            qx[0, h] = q
            qx[1, h] = turned(q.astype(F32), cosine, sine).astype(BF)
        m_s[...] = jnp.full_like(m_s, LOW)
        acc_s[...] = jnp.zeros_like(acc_s)
        any_lo, any_hi = slots, 0
        for c in range(SPANS):
            here = (base < ends[c]) & (base + rows > starts[c])
            some = here & (highs[c] > lows[c])
            any_lo = jnp.where(some, jnp.minimum(any_lo, lows[c]), any_lo)
            any_hi = jnp.where(some, jnp.maximum(any_hi, highs[c]), any_hi)

        def update(which, at, size, mask):
            all_s = [nt_dot(qx[which, h], kk[h, pl.ds(at, size), :]) for h in range(2)]
            all_s = [jnp.where(mask, s_, NEG) for s_ in all_s]
            tops = [jnp.max(s_, axis=1, keepdims=True) for s_ in all_s]
            ps = []
            for h in range(2):
                m_old = m_s[h]
                m_new = jnp.maximum(m_old, tops[h])
                alpha = jnp.exp2((m_old - m_new) * SCALE)
                wide_m = jnp.concatenate([m_new] * (size // HEAD), axis=1)
                ps.append((jnp.exp2((all_s[h] - wide_m) * SCALE).astype(BF), alpha))
                m_s[h] = m_new
            for h in range(2):
                p, alpha = ps[h]
                acc_s[h] = jnp.concatenate([alpha, alpha], axis=1) * acc_s[h] + jnp.dot(
                    p, vv[h, pl.ds(at, size), :], preferred_element_type=F32
                )

        def new_tile(j, carry):
            kb = ((x - j) * Z + z) * rows

            @pl.when((x >= j) & (kb <= base + rows - 1) & (kb + TILE > first_start))
            def _():
                key = kb + lax.broadcasted_iota(I32, (1, TILE), 1)
                update(0, pl.multiple_of(j * TILE, TILE), TILE, (key >= start_q) & (key <= qt))

            return carry

        def old_tile(j, carry):
            kb = j * OLD

            @pl.when((kb < any_hi) & (kb + OLD > any_lo))
            def _():
                key = kb + lax.broadcasted_iota(I32, (1, OLD), 1)
                update(1, pl.multiple_of(old + kb, TILE), OLD, (key >= lo_q) & (key < hi_q))

            return carry

        if fresh:
            lax.fori_loop(0, fresh, new_tile, 0)
        lax.fori_loop(0, (kk.shape[1] - old) // OLD, old_tile, 0)

        lane = lax.broadcasted_iota(I32, (rows, HEAD), 1)
        stats = jnp.zeros((rows, HEAD), F32)
        for h in range(2):
            total = acc_s[h, :, HEAD:]
            inverse = 1.0 / jnp.where(total > 0, total, 1.0)
            msg[s, pl.ds(0, rows), pl.ds(h * HEAD, HEAD)] = (acc_s[h, :, :HEAD] * inverse).astype(BF)
            for k, part in enumerate(pieces(m_s[h], 3) + pieces(total, 2)):
                stats = jnp.where(lane == 5 * h + k, part, stats)
        msg[s, pl.ds(rows, 16), :] = jnp.transpose(stats)[:16].astype(BF)
        found = [d[pl.ds(pl.multiple_of(s * 8, 8), 8), :] for d in dec_refs]
        top = functools.reduce(jnp.maximum, [f[:, HEAD : HEAD + 1] for f in found])
        found = [f * jnp.exp2((f[:, HEAD : HEAD + 1] - top) * SCALE) for f in found]
        part = functools.reduce(jnp.add, found)
        total = part[:, HEAD + 1 : HEAD + 2]
        inverse = 1.0 / jnp.where(total > 0, total, 1.0)
        lane = lax.broadcasted_iota(I32, (8, HEAD), 1)
        stats = jnp.zeros((8, HEAD), F32)
        for k, piece in enumerate(pieces(top, 3) + pieces(total, 2)):
            stats = jnp.where(lane == k, piece, stats)
        part = jnp.concatenate([part[:, :HEAD] * inverse, stats], axis=1)
        msg[s, pl.ds(rows + 16, 16), :] = jnp.concatenate(
            [part, jnp.zeros_like(part)], axis=0
        ).astype(BF)
        for k in range(nq):
            @pl.when(s == k)
            def _():
                pltpu.make_async_copy(msg.at[k], out_refs[k], o_sem.at[k]).start()
        return carry

    lax.fori_loop(0, nq, block, 0)
    for s in range(nq):
        pltpu.make_async_copy(msg.at[s], out_refs[s], o_sem.at[s]).wait()


def attend(lens, sc, turn, dec, queries, fresh, caches):
    rows = fresh[0].shape[2] if fresh else TILE
    slots = caches[0].shape[1] // 2
    keys = len(fresh) * rows + -(-slots // OLD) * OLD
    any_spec = pl.BlockSpec(memory_space=pl.ANY)
    operands = (*queries, *fresh, *caches)
    nf = len(fresh)
    return pl.pallas_call(
        functools.partial(attend_kernel, rows, slots, nf),
        out_shape=[jax.ShapeDtypeStruct((rows + 32, 2 * HEAD), BF)] * Z,
        in_specs=[
            pl.BlockSpec(memory_space=pltpu.SMEM),
            pl.BlockSpec(memory_space=pltpu.SMEM),
        ]
        + [pl.BlockSpec(memory_space=pltpu.VMEM)] * (1 + X)
        + [any_spec] * len(operands),
        out_specs=[any_spec] * Z,
        scratch_shapes=[
            pltpu.VMEM((Z, 2 * rows, HEAD), BF),
            pltpu.VMEM((2, 2, rows, HEAD), BF),
            pltpu.VMEM((2, keys, HEAD), BF),
            pltpu.VMEM((2, keys, 2 * HEAD), BF),
            pltpu.VMEM((2, 2 * slots, HEAD), BF),
            pltpu.VMEM((2 * (slots // 5), HEAD), F32),
            pltpu.VMEM((Z, rows + 32, 2 * HEAD), BF),
            pltpu.VMEM((2, rows, HEAD), F32),
            pltpu.VMEM((2, rows, 2 * HEAD), F32),
            pltpu.SemaphoreType.DMA((Z,)),
            pltpu.SemaphoreType.DMA((max(2 * nf, 1),)),
            pltpu.SemaphoreType.DMA((max(2 * nf, 1),)),
            pltpu.SemaphoreType.DMA((2,)),
            pltpu.SemaphoreType.DMA((Z,)),
        ],
        compiler_params=pltpu.CompilerParams(vmem_limit_bytes=40 << 20),
        cost_estimate=pl.CostEstimate(
            flops=6_000_000_000, bytes_accessed=8_000_000, transcendentals=8_000_000
        ),
        name="attend",
    )(lens, sc, turn, *dec, *operands)


def shift(value, axis, size, step):
    return lax.ppermute(value, axis, [(i, (i + step) % size) for i in range(size)])


def layer_norm(inputs, ln_gain, ln_bias):
    values = inputs.astype(F32)
    center = jnp.mean(values, axis=-1, keepdims=True)
    spread = jnp.mean(jnp.square(values - center), axis=-1, keepdims=True)
    return ((values - center) * lax.rsqrt(spread + 1e-05) * ln_gain + ln_bias).astype(BF)


def form_kernel(rows, dec, lens, proj_ref, bias_ref, power_ref, number_ref, *refs):
    q_ref, fresh_ref, first_ref, mine_ref, small = refs
    base = (lax.axis_index("x") * Z + lax.axis_index("z")) * rows
    starts = (lens[0], lens[0] + lens[1])
    step = 64

    def part(i, carry):
        first_row = pl.multiple_of(i * step, step)
        token = base + first_row + lax.broadcasted_iota(I32, (step, 1), 0)
        start = jnp.where(token >= starts[1], starts[1], jnp.where(token >= starts[0], starts[0], 0))
        offset = token - start
        angle = offset.astype(F32) * power_ref[0:1, :]
        cosine, sine = jnp.cos(angle), jnp.sin(angle) * power_ref[1:2, :]
        at = pl.ds(first_row, step)
        for h in range(2):
            q, k, v = (proj_ref[h, j, at, :] + bias_ref[h, j : j + 1, :] for j in range(3))
            q_ref[pl.ds(pl.multiple_of(h * rows + first_row, step), step), :] = turned(
                q, cosine, sine
            ).astype(BF)
            fresh_ref[0, h, at, :] = turned(k, cosine, sine).astype(BF)
            fresh_ref[1, h, at, :] = v.astype(BF)
        return carry

    lax.fori_loop(0, rows // step, part, 0)
    mine_ref[...] = jnp.zeros_like(mine_ref)
    lane = lax.broadcasted_iota(I32, (dec, HEAD), 1)
    for h in range(2):
        q, k, v = (
            (proj_ref[h, j, pl.ds(rows, dec), :] + bias_ref[h, j : j + 1, :]).astype(BF).astype(F32)
            for j in range(3)
        )
        at = pl.ds(h * dec, dec)
        small[at, :] = q
        score = jnp.sum(q * k, axis=1, keepdims=True)
        mine_ref[at, pl.ds(0, HEAD)] = v
        mine_ref[at, pl.ds(HEAD, HEAD)] = jnp.where(
            lane == 0, score, jnp.where(lane == 1, 1.0, 0.0)
        )
    for k in range(2):
        values = number_ref[k : k + 1, :]
        high = jnp.floor(values / 16.0)
        small[pl.ds(4 + 2 * k, 1), :] = high
        small[pl.ds(5 + 2 * k, 1), :] = values - 16.0 * high
    first_ref[...] = small[...].astype(BF)


def form(lens, projected, bias, power, numbers, rows, dec):
    vmem = pl.BlockSpec(memory_space=pltpu.VMEM)
    return pl.pallas_call(
        functools.partial(form_kernel, rows, dec),
        out_shape=[
            jax.ShapeDtypeStruct((2 * rows, HEAD), BF),
            jax.ShapeDtypeStruct((2, 2, rows, HEAD), BF),
            jax.ShapeDtypeStruct((8, HEAD), BF),
            jax.ShapeDtypeStruct((16, 2 * HEAD), F32),
        ],
        in_specs=[pl.BlockSpec(memory_space=pltpu.SMEM)] + [vmem] * 4,
        out_specs=[vmem] * 4,
        scratch_shapes=[pltpu.VMEM((8, HEAD), F32)],
        cost_estimate=pl.CostEstimate(
            flops=5_000_000, bytes_accessed=1_300_000, transcendentals=70_000
        ),
        name="form",
    )(lens, projected, bias, power, numbers)


def pack_kernel(q_ref, *refs):
    rounds, (out_ref, limit_ref, tail) = refs[:X], refs[X:]
    n = q_ref.shape[0]
    out_ref[pl.ds(0, n), :] = q_ref[...]
    tail[...] = jnp.zeros_like(tail)
    counted = jnp.zeros((1, HEAD), F32)
    limits = jnp.zeros((1, HEAD), F32)
    for r, ref in enumerate(rounds):
        m = ref[...].astype(F32)
        tail[pl.ds(8 * r, 4), :] = m[0:4]
        counted += 16.0 * m[4:5] + m[5:6]
        limits += 16.0 * m[6:7] + m[7:8]
    high = jnp.floor(counted / 32.0)
    tail[pl.ds(4, 1), :] = high
    tail[pl.ds(5, 1), :] = counted - 32.0 * high
    out_ref[pl.ds(n, 8 * X), :] = tail[...].astype(BF)
    limit_ref[...] = jnp.broadcast_to(limits, limit_ref.shape).astype(I32)


def pack(q, rounds):
    return pl.pallas_call(
        pack_kernel,
        out_shape=[
            jax.ShapeDtypeStruct((q.shape[0] + 8 * X, HEAD), BF),
            jax.ShapeDtypeStruct((8, HEAD), I32),
        ],
        scratch_shapes=[pltpu.VMEM((8 * X, HEAD), F32)],
        cost_estimate=pl.CostEstimate(flops=10_000, bytes_accessed=280_000, transcendentals=0),
        name="pack",
    )(q, *rounds)


def decode_kernel(start, dec, group_ref, power_ref, owner_ref, kv_ref, *refs):
    msgs, refs = refs[:Z], refs[Z:]
    outs, refs = refs[:X], refs[X:]
    turn_ref, count_ref, rows_s, q_s, angle_s, label_s, sem = refs
    copies = [
        pltpu.make_async_copy(m.at[pl.ds(start, 8 * X)], rows_s.at[s], sem.at[s])
        for s, m in enumerate(msgs)
    ]
    for c in copies:
        c.start()
    for c in copies:
        c.wait()
    n = Z * X * 8
    rows = rows_s[...].astype(F32).reshape(n, HEAD)
    counts = jnp.zeros((1, HEAD), F32)
    for s in range(Z):
        at = s * X * 8 + 4
        counts += 32.0 * rows[at : at + 1] + rows[at + 1 : at + 2]
    count_ref[...] = jnp.broadcast_to(counts, count_ref.shape)
    row = lax.broadcasted_iota(I32, (n, 1), 0)
    inner = row & 7
    from_r, from_s = (row >> 3) & (X - 1), row >> 5
    x, z = lax.axis_index("x"), lax.axis_index("z")
    request = (((x - from_r + X) & (X - 1)) * Z + ((z - from_s + Z) & (Z - 1))) * dec
    request = request + (inner & (dec - 1))
    head = jnp.where(inner >= dec, 1, 0)
    numbers = lax.broadcasted_iota(I32, (1, group_ref.shape[1]), 1)
    group = jnp.sum(jnp.where(numbers == request, group_ref[...], 0), axis=1, keepdims=True)
    real = inner < 2 * dec
    first = jnp.where(real, SPANS + group, -7)
    second = jnp.where(real, SPANS + GROUPS + request, -7)
    span = lax.broadcasted_iota(I32, (16, 1), 0)
    lanes = lax.broadcasted_iota(I32, (1, HEAD), 1)
    picked = (lanes == jnp.concatenate([first, span], axis=0)) | (
        lanes == jnp.concatenate([second, span], axis=0)
    )
    position = jnp.sum(jnp.where(picked, counts, 0.0), axis=1, keepdims=True)
    angle = position * power_ref[0:1, :]
    span_angle = angle[n : n + 8]
    turn_ref[0:4, :] = jnp.cos(span_angle)[0:4]
    turn_ref[4:8, :] = (jnp.sin(span_angle) * power_ref[1:2, :])[0:4]
    q_s[...] = rows
    angle_s[...] = angle[:n]
    lane = lax.broadcasted_iota(I32, (n, HEAD), 1)
    label_s[...] = jnp.where(lane == 0, first, jnp.where(lane == 1, second, head))
    owner = owner_ref[...]
    parity = lax.broadcasted_iota(I32, owner.shape, 1) & 1
    step = 2 * X * 8

    def some(i, carry):
        at = pl.ds(pl.multiple_of(i * step, step), step)
        labels = label_s[at, :]
        mask = ((owner == labels[:, 0:1]) | (owner == labels[:, 1:2])) & (parity == labels[:, 2:3])
        angle = angle_s[at, :]
        q = turned(q_s[at, :], jnp.cos(angle), jnp.sin(angle) * power_ref[1:2, :]).astype(BF)
        scores = jnp.where(mask, nt_dot(q, kv_ref[0]), NEG)
        top = jnp.maximum(jnp.max(scores, axis=1, keepdims=True), LOW)
        p = jnp.exp2((scores - top) * SCALE)
        lane = lax.broadcasted_iota(I32, (step, HEAD), 1)
        total = jnp.sum(p, axis=1, keepdims=True)
        stats = jnp.where(lane == 0, top, jnp.where(lane == 1, total, 0.0))
        mixed = jnp.dot(p.astype(BF), kv_ref[1], preferred_element_type=F32)
        for s in range(2):
            to = pl.ds(pl.multiple_of(i * 16 + s * 8, 8), 8)
            for r in range(X):
                row = (s * X + r) * 8
                outs[r][to, pl.ds(0, HEAD)] = mixed[row : row + 8]
                outs[r][to, pl.ds(HEAD, HEAD)] = stats[row : row + 8]
        return carry

    lax.fori_loop(0, n // step, some, 0)


def decode_attend(start, dec, group, power, owner, kv, msgs):
    vmem = pl.BlockSpec(memory_space=pltpu.VMEM)
    out = pl.pallas_call(
        functools.partial(decode_kernel, start, dec),
        out_shape=[jax.ShapeDtypeStruct((Z * 8, 2 * HEAD), F32)] * X
        + [jax.ShapeDtypeStruct((8, HEAD), F32)] * 2,
        in_specs=[vmem] * 4 + [pl.BlockSpec(memory_space=pl.ANY)] * Z,
        out_specs=[vmem] * (X + 2),
        scratch_shapes=[
            pltpu.VMEM((Z, 8 * X, HEAD), BF),
            pltpu.VMEM((Z * X * 8, HEAD), F32),
            pltpu.VMEM((Z * X * 8, HEAD), F32),
            pltpu.VMEM((Z * X * 8, HEAD), I32),
            pltpu.SemaphoreType.DMA((Z,)),
        ],
        cost_estimate=pl.CostEstimate(
            flops=220_000_000, bytes_accessed=1_500_000, transcendentals=500_000
        ),
        name="decode_attend",
    )(group, power, owner, kv, *msgs)
    return out[:X], out[X], out[X + 1]


def combine_kernel(rows, dec, self_ref, *refs):
    msgs, out_ref, columns = refs[:-2], refs[-2], refs[-1]
    n = len(msgs)
    stats = [m[pl.ds(rows, 16), :].astype(F32) for m in msgs]
    weights = []
    for h in range(2):
        tops = [
            s[5 * h : 5 * h + 1] + s[5 * h + 1 : 5 * h + 2] + s[5 * h + 2 : 5 * h + 3]
            for s in stats
        ]
        totals = [s[5 * h + 3 : 5 * h + 4] + s[5 * h + 4 : 5 * h + 5] for s in stats]
        top = functools.reduce(jnp.maximum, tops)
        shares = [t * jnp.exp2((m - top) * SCALE) for m, t in zip(tops, totals)]
        inverse = 1.0 / functools.reduce(jnp.add, shares)
        weights += [s * inverse for s in shares]
    table = jnp.concatenate(weights + [jnp.zeros((HEAD - 2 * n, rows), F32)], axis=0)
    columns[...] = jnp.transpose(table)
    step = 64

    def part(j, carry):
        at = pl.ds(pl.multiple_of(j * step, step), step)
        shares = columns[at, :]
        for h in range(2):
            side = pl.ds(h * HEAD, HEAD)
            total = jnp.zeros((step, HEAD), F32)
            for i, m in enumerate(msgs):
                k = h * n + i
                total += shares[:, k : k + 1] * m[at, side].astype(F32)
            out_ref[at, side] = total.astype(BF)
        return carry

    lax.fori_loop(0, rows // step, part, 0)

    values, tops, totals = [], [], []
    for m in msgs:
        part = m[pl.ds(rows + 16, 16), :].astype(F32)
        values.append(part[:, :HEAD])
        tops.append(
            part[:, HEAD : HEAD + 1] + part[:, HEAD + 1 : HEAD + 2] + part[:, HEAD + 2 : HEAD + 3]
        )
        totals.append(part[:, HEAD + 3 : HEAD + 4] + part[:, HEAD + 4 : HEAD + 5])
    mine = self_ref[...]
    values.append(mine[:, :HEAD])
    tops.append(mine[:, HEAD : HEAD + 1])
    totals.append(mine[:, HEAD + 1 : HEAD + 2])
    top = functools.reduce(jnp.maximum, tops)
    shares = [t * jnp.exp2((m - top) * SCALE) for m, t in zip(tops, totals)]
    whole = functools.reduce(jnp.add, shares)
    mixed = functools.reduce(jnp.add, [s * v for s, v in zip(shares, values)])
    mixed = mixed / jnp.where(whole > 0, whole, 1.0)
    out_ref[pl.ds(rows, 16), :HEAD] = mixed.astype(BF)
    out_ref[pl.ds(rows, 16), HEAD:] = pltpu.roll(mixed, 16 - dec, 0).astype(BF)


def combine(mine, msgs, dec):
    rows = msgs[0].shape[0] - 32
    return pl.pallas_call(
        functools.partial(combine_kernel, rows, dec),
        out_shape=jax.ShapeDtypeStruct((rows + 16, 2 * HEAD), BF),
        scratch_shapes=[pltpu.VMEM((rows, HEAD), F32)],
        cost_estimate=pl.CostEstimate(
            flops=2_000_000, bytes_accessed=1_300_000, transcendentals=10_000
        ),
        name="combine",
    )(mine, *msgs)


def project_kernel(*refs):
    parts, refs = refs[: 2 * Y], refs[2 * Y :]
    w_ref, bias_ref, out_ref, dec_ref = refs
    y, core = lax.axis_index("y"), lax.axis_index("core")
    step = 256

    def part(j, carry):
        at = pl.ds(pl.multiple_of(j * step, step), step)
        total = jnp.zeros((parts[0].shape[0], step), F32)
        for k, part in enumerate(parts):
            r, c = k % Y, k // Y
            owner = lax.rem(y - r + Y, Y) * C + lax.rem(core + c, C)
            total += jnp.dot(part[...], w_ref[owner, :, at], preferred_element_type=F32)
        total = (total + bias_ref[:, at]).astype(BF)
        out_ref[:, at] = total[: out_ref.shape[0]]
        dec_ref[:, at] = total[out_ref.shape[0] :][: dec_ref.shape[0]]
        return carry

    lax.fori_loop(0, out_ref.shape[1] // step, part, 0)


def project(parts, w, bias, rows, dec):
    vmem = pl.BlockSpec(memory_space=pltpu.VMEM)
    return pl.pallas_call(
        project_kernel,
        out_shape=[
            jax.ShapeDtypeStruct((rows, w.shape[2]), BF),
            jax.ShapeDtypeStruct((dec, w.shape[2]), BF),
        ],
        in_specs=[vmem] * (2 * Y + 2),
        out_specs=[vmem, vmem],
        cost_estimate=pl.CostEstimate(
            flops=550_000_000, bytes_accessed=3_500_000, transcendentals=0
        ),
        name="project",
    )(*parts, w, bias)


def column_kernel(w_ref, out_ref):
    out_ref[0] = w_ref[...]


def columns_of(w, parts):
    rows, width = w.shape[0], w.shape[1] // parts
    return pl.pallas_call(
        column_kernel,
        grid=(parts,),
        out_shape=jax.ShapeDtypeStruct((parts, rows, width), BF),
        in_specs=[pl.BlockSpec((rows, width), lambda j: (0, j))],
        out_specs=pl.BlockSpec((1, rows, width), lambda j: (j, 0, 0)),
        cost_estimate=pl.CostEstimate(flops=0, bytes_accessed=4_200_000, transcendentals=0),
        name="columns_of",
    )(w)


def merge_messages(a, b, rows):
    def parse(m):
        stats = m[:, rows : rows + 16].astype(F32)
        out = []
        for h in range(2):
            s = stats[:, 5 * h : 5 * h + 5]
            out.append((s[:, 0] + s[:, 1] + s[:, 2], s[:, 3] + s[:, 4]))
        return out

    results, stat_rows = [], []
    for h, ((ma, la), (mb, lb)) in enumerate(zip(parse(a), parse(b))):
        top = jnp.maximum(ma, mb)
        wa = la * jnp.exp2((ma - top) * SCALE)
        wb = lb * jnp.exp2((mb - top) * SCALE)
        total = wa + wb
        inverse = 1.0 / jnp.where(total > 0, total, 1.0)
        part = slice(h * HEAD, (h + 1) * HEAD)
        results.append(
            (wa * inverse)[..., None] * a[:, :rows, part].astype(F32)
            + (wb * inverse)[..., None] * b[:, :rows, part].astype(F32)
        )
        for value, count in ((top, 3), (total, 2)):
            for _ in range(count):
                piece = lax.reduce_precision(value, 8, 7)
                stat_rows.append(piece)
                value = value - piece
    stat_rows += [jnp.zeros_like(stat_rows[0])] * 6
    return jnp.concatenate(
        [
            jnp.concatenate(results, axis=2).astype(BF),
            jnp.stack(stat_rows, axis=1).astype(BF),
            a[:, rows + 16 :],
        ],
        axis=1,
    )


def on_device(
    prefill_x,
    decode_x,
    ln_gain,
    ln_bias,
    wqkv,
    qkv_bias,
    dense_w,
    dense_bias,
    kv_cache,
    slot_owner,
    group_of,
    span_lens,
):
    x = lax.axis_index("x")
    rows, dec = prefill_x.shape[0], decode_x.shape[0]
    slots = slot_owner.shape[0]
    requests = group_of.shape[0]
    owners = SPANS + GROUPS + requests
    cache = kv_cache.reshape(2, 2 * slots, HEAD)

    owner_ids = jnp.arange(HEAD, dtype=I32)
    hits = (slot_owner[:, None] == owner_ids[None, :]) & (owner_ids < owners)[None, :]
    local = jnp.sum(hits.astype(F32), axis=0)
    begin = jnp.min(
        jnp.where(hits[:, :SPANS], jnp.arange(slots, dtype=I32)[:, None], slots), axis=0
    ).astype(F32)
    bounds = jnp.concatenate([begin, begin + local[:SPANS]])
    extra = jnp.where(x > 0, jnp.sum(local[:SPANS]), 0.0)
    vector = jnp.where(owner_ids == HEAD - 1, extra, local)
    at_row = jnp.where(x == 0, jnp.pad(bounds, (0, HEAD - 2 * SPANS)), 0.0)
    numbers = jnp.stack([vector, at_row])

    power = jnp.power(F32(10000.0), jnp.arange(ROT // 2, dtype=F32) * (-2.0 / ROT))
    lane = jnp.arange(HEAD, dtype=I32)
    power_lanes = jnp.where(lane < ROT, jnp.tile(power, HEAD // (ROT // 2)), 0.0)
    power_rows = jnp.stack([power_lanes, jnp.where(lane < ROT // 2, -1.0, 1.0).astype(F32)])
    normed = layer_norm(jnp.concatenate([prefill_x, decode_x], axis=0), ln_gain, ln_bias)
    projected = jnp.einsum("td,dhje->hjte", normed, wqkv, preferred_element_type=F32)
    my_q, fresh, first, mine = form(span_lens, projected, qkv_bias, power_rows, numbers, rows, dec)

    rounds = [first] + [shift(first, "x", X, r) for r in range(1, X)]
    cache_sent, _ = lax.optimization_barrier((cache, first))
    cache_1 = lax.ppermute(cache_sent, "x", [(0, 1)])
    cache_3 = lax.ppermute(cache_sent, "x", [(0, 3)])

    second, limits = pack(my_q, rounds)
    second, fresh = lax.optimization_barrier((second, fresh))
    all_q = [second] + [shift(second, "z", Z, s) for s in range(1, Z)]
    all_kv = [fresh] + [
        lax.ppermute(fresh, "x", [(i, i + r) for i in range(X - r)]) for r in (1, 2)
    ]
    half_1, half_3 = lax.optimization_barrier((cache_1[0], cache_3[1]))
    cache_2k = lax.ppermute(half_1, "x", [(1, 2)])
    cache_2v = lax.ppermute(half_3, "x", [(3, 2)])

    late_owner, late_group, _ = lax.optimization_barrier((slot_owner, group_of, second))
    owner_row = jnp.repeat(late_owner, 2)[None, :]
    ready = lax.optimization_barrier((tuple(all_q), cache_2k, cache_2v))
    all_q, cache_2k, cache_2v = ready
    parts, turn, counts = decode_attend(
        2 * rows, dec, late_group[None, :], power_rows, owner_row, cache, all_q
    )
    more = counts[0, HEAD - 1] > 0
    parts = [parts[0]] + [shift(parts[r], "x", X, X - r) for r in range(1, X)]

    held_w, turn = lax.optimization_barrier((dense_w, turn))
    w_out = columns_of(held_w.reshape(2 * HEAD, -1), Y * C)
    w_out, parts[0] = lax.optimization_barrier((w_out, parts[0]))
    w_out = lax.all_to_all(w_out, ("y", "core"), 0, 0)

    def general(msgs):
        def step(i, state):
            msgs, held, limits, row_of = state
            limits_now = jnp.where(row_of > 0, limits, jnp.zeros_like(limits))
            limits_now = jnp.pad(limits_now, (0, HEAD - 2 * SPANS))[None, :]
            five = (held, held, held, held[0], held[1])
            found = attend(span_lens, limits_now, turn, parts, all_q, [], five)
            return (
                merge_messages(msgs, jnp.stack(found), rows),
                shift(held, "x", X, 1),
                shift(limits, "x", X, 1),
                shift(row_of, "x", X, 1),
            )

        state = (jnp.stack(msgs), cache, bounds.astype(I32), x)
        return tuple(lax.fori_loop(0, X, step, state)[0])

    caches = (cache, cache_1, cache_3, cache_2k, cache_2v)
    msgs = tuple(attend(span_lens, limits, turn, parts, all_q, all_kv, caches))
    msgs = lax.while_loop(
        lambda state: state[0],
        lambda state: (jnp.zeros((), bool), general(state[1])),
        (more, msgs),
    )[1]
    home = [msgs[0]] + [shift(msgs[s], "z", Z, Z - s) for s in range(1, Z)]
    attended = combine(mine, home, dec)

    over_y = [attended] + [shift(attended, "y", Y, r) for r in range(1, Y)]
    over_y += [lax.ppermute(v, "core", [(0, 1), (1, 0)]) for v in over_y]
    return tuple(project(over_y, w_out, dense_bias[None, :], rows, dec))


def solution(mesh):
    mesh = Mesh(mesh.devices.reshape(X, Z, Y, C), ("x", "z", "y", "core"))
    seq, tensor = ("x", "z"), ("y", "core")
    in_specs = (
        P(seq, None),
        P(seq, None),
        P(),
        P(),
        P(None, tensor, None, None),
        P(tensor, None, None),
        P(tensor, None, None),
        P(tensor),
        P(None, seq, tensor, None),
        P(seq),
        P(),
        P(),
    )
    out_specs = (P(seq, tensor), P(seq, tensor))

    return jax.shard_map(
        on_device, mesh=mesh, in_specs=in_specs, out_specs=out_specs, check_vma=False
    )
```
